128 devices in a mesh: ctx: 16 (over z_hi, y, core), exp: 8 (over z_lo, x).
Axes of the slice: x: 4, y: 4, z: 4 (z_hi: 2, z_lo: 2; z = z_hi * 2 + z_lo), core: 2. Of those that a mesh axis runs over, the one named last changes fastest.
Arguments:
- hidden: bfloat16 [16384, 2048], P(('ctx', 'exp')), may hold values from -6 to 6
- queries: bfloat16 [16384, 2048], P(('ctx', 'exp')), may hold values from -16 to 16
- keys: bfloat16 [16384, 256], P(('ctx', 'exp')), may hold values from -4 to 4
- values: bfloat16 [16384, 256], P(('ctx', 'exp')), may hold values from -6 to 6
- w_out: bfloat16 [2048, 2048], replicated, may hold values from -0.125 to 0.125
- norm_gain: float32 [2048], replicated, may hold values from 0.5 to 1.5
- w_router: bfloat16 [2048, 128], replicated, may hold values from -0.125 to 0.125
- expert_ids: int32 [16384, 8], P(('ctx', 'exp')), may hold values from 0 to 127, all different within a row; in each aligned block of 128 rows (0 to 127, 128 to 255, ...) at most 9 rows name the same one
- w_gate: bfloat16 [128, 2048, 768], P(('ctx', 'exp')), may hold values from -0.125 to 0.125
- w_up: bfloat16 [128, 2048, 768], P(('ctx', 'exp')), may hold values from -0.125 to 0.125
- w_down: bfloat16 [128, 768, 2048], P(('ctx', 'exp')), may hold values from -0.21875 to 0.21875
Outputs:
- mixed: bfloat16 [16384, 2048], P(('ctx', 'exp'))
The draws below stay inside these ranges and needn't reach their ends.
Inputs may be any that keep to these rules, and one draw needn't show every extreme that they name: `expert_ids`: within the 128 tokens of one device, no expert is named by more than 9 of their routes, a bound that some block reaches of them; a token's experts are distinct.
All inputs are finite; a program needn't handle non-finite values.
Results may differ from the reference program's by a relative error of at most 0.01.
Values may be sent and summed in bfloat16 or wider, within the bound.
No kernel may reach another device: no remote copies, remote signals or barrier semaphores. Data moves between devices by JAX's collectives and lax.ppermute only.
A program may use at most 192 MiB of HBM per device.

```python
import math
import jax
import jax.numpy as jnp
import numpy as np
from jax import lax

D = 2048
HQ = 16
HK = 2
DH = 128
E = 128
F = 768
TOP = 8
TOK_DEV = 128
TOKENS = 16384
CAP = 9


def joint_draw(key):
    key_query = jax.random.fold_in(key, 101)
    key_keys = jax.random.fold_in(key, 202)
    keys_f = jnp.clip(jax.random.normal(key_keys, (TOKENS, HK * DH), jnp.float32), -4.0, 4.0)
    query_f = jnp.clip(jax.random.normal(key_query, (TOKENS, HQ * DH), jnp.float32), -4.0, 4.0)
    return (query_f, keys_f)


def draw_queries(key, part):
    return joint_draw(key)[0].astype(jnp.bfloat16)


def draw_keys(key, part):
    return joint_draw(key)[1].astype(jnp.bfloat16)


def block_levels(own_key, shape, cuts, smallest, largest):
    gain = 1.0
    for dim, blocks in cuts:
        heights = jax.random.uniform(jax.random.fold_in(jax.random.fold_in(own_key, 6), dim), (blocks,), jnp.float32, smallest / len(cuts), largest / len(cuts))
        gain = gain * jnp.repeat(jnp.exp(heights), shape[dim] // blocks).reshape((-1,) + (1,) * (len(shape) - 1 - dim))
    return gain


def routed_block(own_key, own, number, rows, amount, top, bound, lean):
    order = jax.random.permutation(own_key, amount)
    crowded, common = portions_of(amount, rows * top, bound, lean, True), portions_of(amount, rows * top, bound, lean, False)
    places = jnp.arange(amount)

    def named(lengths, offset_by):
        used = int((lengths > 0).sum())
        fixed = max(1, used // 4)
        passed = fixed + (places - fixed + offset_by * (used - fixed)) % max(1, amount - fixed)
        return jnp.zeros((amount,), jnp.int32).at[order[jnp.where(places < fixed, places, passed)]].set(jnp.asarray(lengths, jnp.int32))

    lengths = jnp.where(number % 4 == 0, named(crowded, number // 4), named(common, number - number // 4 - 1))
    mixed = jax.random.permutation(jax.random.fold_in(own, 3), amount)
    giver, sink = mixed[0:amount // 2 * 2:2], mixed[1:amount // 2 * 2:2]
    slack = jnp.minimum(lengths[giver] - 1, bound - lengths[sink]) // 2
    slack = jnp.where((giver == order[0]) | (sink == order[0]) | (lengths[sink] == 0), 0, jnp.maximum(slack, 0))
    passed = jax.random.randint(jax.random.fold_in(own, 4), (amount // 2,), 0, 1 << 20) % (slack + 1)
    lengths = lengths.at[giver].add(-passed).at[sink].add(passed)
    labels = jnp.searchsorted(jnp.cumsum(lengths), jnp.arange(rows * top), side="right").astype(jnp.int32)
    grid = labels.reshape(top, rows).T
    grid = grid[jax.random.permutation(jax.random.fold_in(own, 1), rows)]
    offset_by = jax.random.randint(jax.random.fold_in(own, 2), (rows, 1), 0, top)
    return jnp.take_along_axis(grid, (jnp.arange(top)[None, :] + offset_by) % top, axis=1)


def portions_of(count, total, most, lean, full):
    loads = [(1 << 20) // math.isqrt(grade ** lean) + 1 for grade in range(1, count + 1)]
    largest = most if full else min(most, max(-(-total // count), total * loads[0] // sum(loads)))
    least = 1 if total - largest >= count - 1 else 0
    given, spare = [largest] + [least] * (count - 1), total - largest - least * (count - 1)
    while spare > 0:
        free = [i for i in range(1, count) if given[i] < largest] or [i for i in range(1, count) if given[i] < most]
        pool, budget = sum([loads[i] for i in free]), spare
        for i in free:
            extra = min(most - given[i], max(1, budget * loads[i] // pool), spare)
            given[i] = given[i] + extra
            spare = spare - extra
    return np.array(given)


def gaussian(stream_key, shape, deviation, most, pieces=(), kind=jnp.bfloat16):
    entries = deviation * jax.random.normal(stream_key, shape, jnp.float32)
    if pieces:
        entries = entries * block_levels(stream_key, shape, pieces, -0.22, 0.18)
    return jnp.clip(entries, -most, most).astype(kind)


def setup_inputs(seed: int = 0) -> dict:
    streams_of = jax.random.split(jax.random.key(seed), 12)
    hidden = gaussian(streams_of[0], (TOKENS, D), 1.0, 6.0, ((0, 128),))
    queries = draw_queries(jax.random.fold_in(streams_of[11], 71), 0)
    keys = draw_keys(jax.random.fold_in(streams_of[11], 71), 0)
    values = gaussian(streams_of[3], (TOKENS, HK * DH), 1.0, 6.0, ((0, 128),))
    w_out = gaussian(streams_of[4], (HQ * DH, D), (HQ * DH) ** -0.5, 0.125)
    norm_gain = jnp.clip(1.0 + 0.1 * jax.random.normal(streams_of[5], (D,), jnp.float32), 0.5, 1.5)
    w_router = gaussian(streams_of[6], (D, E), D ** -0.5, 0.125)
    expert_ids_keys = jax.random.split(jax.random.fold_in(streams_of[7], 1), TOKENS // TOK_DEV)
    expert_ids_turns = jax.random.permutation(jax.random.fold_in(streams_of[7], 3), TOKENS // TOK_DEV)
    expert_ids = jax.vmap(lambda own, number: routed_block(jax.random.fold_in(streams_of[7], 2), own, number, TOK_DEV, E, TOP, CAP, 2))(expert_ids_keys, expert_ids_turns).reshape((TOKENS, TOP))
    w_gate = gaussian(streams_of[8], (E, D, F), D ** -0.5, 0.125, ((0, 128),))
    w_up = gaussian(streams_of[9], (E, D, F), D ** -0.5, 0.125, ((0, 128),))
    w_down = gaussian(streams_of[10], (E, F, D), F ** -0.5, 0.21875, ((0, 128),))
    return dict(hidden=hidden, queries=queries, keys=keys, values=values, w_out=w_out, norm_gain=norm_gain, w_router=w_router, expert_ids=expert_ids, w_gate=w_gate, w_up=w_up, w_down=w_down)


rope_base = 1000000.0
yarn_factor = 4.0
orig_len = 32768.0
beta_fast = 32.0
beta_slow = 1.0
mscale_yarn = 0.1 * math.log(4.0) + 1.0

def yarn_tables(positions, head_size):
    half_size = head_size // 2
    index_f = jnp.arange(half_size, dtype=jnp.float32)
    pos_freq = rope_base ** (2.0 * index_f / head_size)
    inv_extra = 1.0 / pos_freq
    inv_inter = 1.0 / (yarn_factor * pos_freq)
    low_dim = max(math.floor(head_size * math.log(orig_len / (beta_fast * 2.0 * math.pi)) / (2.0 * math.log(rope_base))), 0)
    high_dim = min(math.ceil(head_size * math.log(orig_len / (beta_slow * 2.0 * math.pi)) / (2.0 * math.log(rope_base))), head_size - 1)
    ramp_part = jnp.clip((index_f - low_dim) / max(high_dim - low_dim, 0.001), 0.0, 1.0)
    extra_part = 1.0 - ramp_part
    inverse = inv_inter * (1.0 - extra_part) + inv_extra * extra_part
    angles = positions.astype(jnp.float32)[:, None] * inverse[None, :]
    angles = jnp.concatenate([angles, angles], axis=-1)
    return (jnp.cos(angles) * mscale_yarn, jnp.sin(angles) * mscale_yarn)

def rotate(vectors, cos_table, sin_table):
    values_f = vectors.astype(jnp.float32)
    half_size = values_f.shape[-1] // 2
    turned = jnp.concatenate([-values_f[..., half_size:], values_f[..., :half_size]], axis=-1)
    return (values_f * cos_table[:, None, :] + turned * sin_table[:, None, :]).astype(jnp.bfloat16)

def reference(hidden, queries, keys, values, w_out, norm_gain, w_router, expert_ids, w_gate, w_up, w_down):
    group = HQ // HK
    block_rows = math.gcd(TOKENS, 256)
    positions = jnp.arange(TOKENS, dtype=jnp.int32)
    cos_table, sin_table = yarn_tables(positions, DH)
    q_rot = rotate(queries.reshape(TOKENS, HQ, DH), cos_table, sin_table)
    q_blocks = q_rot.reshape(TOKENS // block_rows, block_rows, HK, group, DH)
    k_rot = rotate(keys.reshape(TOKENS, HK, DH), cos_table, sin_table).astype(jnp.float32)
    v_all = values.reshape(TOKENS, HK, DH).astype(jnp.float32)
    key_rows = jnp.arange(TOKENS, dtype=jnp.int32)
    block_starts = jnp.arange(TOKENS // block_rows, dtype=jnp.int32) * block_rows
    scale = 1.0 / math.sqrt(DH)

    def attend(operands):
        q_block, q_start = operands
        scores = jnp.einsum('thgd,phd->thgp', q_block.astype(jnp.float32), k_rot) * scale
        q_rows = q_start + jnp.arange(block_rows, dtype=jnp.int32)
        allowed = (key_rows[None, :] <= q_rows[:, None])[:, None, None, :]
        scores = jnp.where(allowed, scores, -1e+30)
        peak = lax.optimization_barrier(jnp.max(scores, axis=-1, keepdims=True))
        weights = jnp.where(allowed, jnp.exp(scores - peak), 0.0)
        total = lax.optimization_barrier(jnp.sum(weights, axis=-1))
        rounded = lax.optimization_barrier(weights.astype(jnp.bfloat16))
        summed = jnp.einsum('thgp,phd->thgd', rounded.astype(jnp.float32), v_all)
        return (summed / total[..., None]).astype(jnp.bfloat16).reshape(block_rows, HQ * DH)
    attn = lax.map(attend, (q_blocks, block_starts)).reshape(TOKENS, HQ * DH)
    h1 = (jnp.dot(attn, w_out, preferred_element_type=jnp.float32) + hidden.astype(jnp.float32)).astype(jnp.bfloat16)
    h1_f = h1.astype(jnp.float32)
    normed = h1_f / jnp.sqrt(lax.optimization_barrier(jnp.mean(h1_f * h1_f, axis=-1, keepdims=True)) + 1e-06) * norm_gain[None, :]
    hn = normed.astype(jnp.bfloat16)
    logits = jnp.dot(hn, w_router, preferred_element_type=jnp.float32)
    chosen = jnp.take_along_axis(logits, expert_ids, axis=1)
    raised = jnp.exp(chosen)
    route_w = (raised / lax.optimization_barrier(jnp.sum(raised, axis=-1, keepdims=True))).astype(jnp.bfloat16)
    num_blocks = TOKENS // TOK_DEV
    onehot = (expert_ids[:, :, None] == jnp.arange(E, dtype=jnp.int32)[None, None, :]).astype(jnp.int32)
    counts = jnp.cumsum(onehot.reshape(num_blocks, TOK_DEV * TOP, E), axis=1).reshape(TOKENS, TOP, E)
    slot = lax.optimization_barrier(jnp.sum(onehot * counts, axis=-1)) - 1
    token_ids = jnp.arange(TOKENS, dtype=jnp.int32)
    buffer_row = ((token_ids // TOK_DEV)[:, None] * CAP + slot).astype(jnp.int32)
    table = jnp.full((E, num_blocks * CAP), TOKENS, dtype=jnp.int32)
    table = table.at[expert_ids, buffer_row].set(jnp.broadcast_to(token_ids[:, None], (TOKENS, TOP)))
    hn_pad = jnp.concatenate([hn, jnp.zeros((1, D), jnp.bfloat16)], axis=0)

    def expert(operands):
        index_rows, gate_e, up_e, down_e = operands
        inputs_rows = hn_pad[index_rows]
        gate_v = jnp.dot(inputs_rows, gate_e, preferred_element_type=jnp.float32)
        up_v = jnp.dot(inputs_rows, up_e, preferred_element_type=jnp.float32)
        active = (jax.nn.silu(gate_v) * up_v).astype(jnp.bfloat16)
        return jnp.dot(active, down_e, preferred_element_type=jnp.float32).astype(jnp.bfloat16)
    outputs = lax.map(expert, (table, w_gate, w_up, w_down))
    total_out = h1_f
    for choice_k in range(TOP):
        picked = outputs[expert_ids[:, choice_k], buffer_row[:, choice_k]].astype(jnp.float32)
        total_out = total_out + route_w[:, choice_k].astype(jnp.float32)[:, None] * picked
    return total_out.astype(jnp.bfloat16)
```

```python
import functools
import math

import jax
import jax.numpy as jnp
from jax import lax
from jax.experimental import pallas as pl
from jax.experimental.pallas import tpu as pltpu
from jax.sharding import Mesh, PartitionSpec as P

DH = 128
TOP = 8
CAP = 9
MAIN = 8
BLOCK = 128
BLOCKS = 128
CHUNK_BLOCKS = 8
AXES = ("zh", "y", "c", "zl", "x")
TORUS = ("zh", "zl", "y", "x", "c")

rope_base = 1000000.0
yarn_factor = 4.0
orig_len = 32768.0
beta_fast = 32.0
beta_slow = 1.0
mscale_yarn = 0.1 * math.log(4.0) + 1.0

F32 = jnp.float32
BF16 = jnp.bfloat16
VMEM_LIMIT = 60 * 1024 * 1024


def params(*semantics):
    return pltpu.CompilerParams(
        dimension_semantics=semantics, vmem_limit_bytes=VMEM_LIMIT
    )


def yarn_tables(positions, head_size):
    half_size = head_size // 2
    index_f = jnp.arange(half_size, dtype=jnp.float32)
    pos_freq = rope_base ** (2.0 * index_f / head_size)
    inv_extra = 1.0 / pos_freq
    inv_inter = 1.0 / (yarn_factor * pos_freq)
    low_dim = max(
        math.floor(
            head_size
            * math.log(orig_len / (beta_fast * 2.0 * math.pi))
            / (2.0 * math.log(rope_base))
        ),
        0,
    )
    high_dim = min(
        math.ceil(
            head_size
            * math.log(orig_len / (beta_slow * 2.0 * math.pi))
            / (2.0 * math.log(rope_base))
        ),
        head_size - 1,
    )
    ramp_part = jnp.clip((index_f - low_dim) / max(high_dim - low_dim, 0.001), 0.0, 1.0)
    extra_part = 1.0 - ramp_part
    inverse = inv_inter * (1.0 - extra_part) + inv_extra * extra_part
    angles = positions.astype(jnp.float32)[:, None] * inverse[None, :]
    cos_half = jnp.cos(angles) * mscale_yarn
    sin_half = jnp.sin(angles) * mscale_yarn
    return (
        jnp.concatenate([cos_half, cos_half], axis=-1),
        jnp.concatenate([-sin_half, sin_half], axis=-1),
    )


def rotate_kernel(core_ref, q_ref, k_ref, v_ref, cos_ref, sin_ref, keep_ref, give_ref, kv_ref):
    core = core_ref[0]
    cos_t = cos_ref[...]
    sin_t = sin_ref[...]

    def rotated(part):
        value = part.astype(F32)
        return (value * cos_t + pltpu.roll(value, DH // 2, 1) * sin_t).astype(BF16)

    for head in range(2):
        columns = pl.ds(head * DH, DH)
        kv_ref[:, columns] = rotated(k_ref[:, columns])
    kv_ref[:, pl.ds(2 * DH, 2 * DH)] = v_ref[...]
    half = keep_ref.shape[1]
    for out_ref, which in ((keep_ref, core), (give_ref, 1 - core)):
        for head in range(half // DH):
            source = pl.ds(pl.multiple_of(which * half + head * DH, DH), DH)
            out_ref[:, pl.ds(head * DH, DH)] = rotated(q_ref[:, source])


def rotate_all(core, queries, keys, values, cos_t, sin_t):
    rows, width = queries.shape
    vmem = pl.BlockSpec(memory_space=pltpu.VMEM)
    return pl.pallas_call(
        rotate_kernel,
        in_specs=[pl.BlockSpec(memory_space=pltpu.SMEM)] + [vmem] * 5,
        out_specs=[vmem] * 3,
        out_shape=[
            jax.ShapeDtypeStruct((rows, width // 2), BF16),
            jax.ShapeDtypeStruct((rows, width // 2), BF16),
            jax.ShapeDtypeStruct((rows, 4 * DH), BF16),
        ],
        compiler_params=params(),
        name="rotate_all",
    )(core, queries, keys, values, cos_t, sin_t)


def attend_kernel(
    meta_ref, q_ref, k_ref, v_ref, out_ref, max_ref, sum_ref, acc_ref, *, heads, tile_heads
):
    step = pl.program_id(0)
    first_steps = meta_ref[2]
    second = step >= first_steps
    chunk = jnp.where(second, step - first_steps, step)
    block = jnp.where(second, meta_ref[1], meta_ref[0])
    diagonal = block // CHUNK_BLOCKS
    keys_len = CHUNK_BLOCKS * BLOCK
    factor = math.log2(math.e) / math.sqrt(DH)
    rows = tile_heads * BLOCK

    @pl.when(chunk == 0)
    def _():
        max_ref[...] = jnp.full_like(max_ref, -1e30)
        sum_ref[...] = jnp.zeros_like(sum_ref)
        acc_ref[...] = jnp.zeros_like(acc_ref)

    def update(masked):
        keys = k_ref[...].reshape(keys_len, DH)
        vals = v_ref[...].reshape(keys_len, DH)
        if masked:
            offset = (block - chunk * CHUNK_BLOCKS) * BLOCK
            row_token = lax.broadcasted_iota(jnp.int32, (BLOCK, keys_len), 0) + offset
            key_token = lax.broadcasted_iota(jnp.int32, (BLOCK, keys_len), 1)
            allowed = key_token <= row_token
        for part in range(heads // tile_heads):
            span = pl.ds(part * rows, rows)
            query = jnp.concatenate(
                [
                    q_ref[0, :, pl.ds((part * tile_heads + h) * DH, DH)]
                    for h in range(tile_heads)
                ],
                axis=0,
            )
            scores = lax.dot_general(
                query, keys, (((1,), (1,)), ((), ())), preferred_element_type=F32
            )
            if masked:
                scores = jnp.where(
                    allowed[None], scores.reshape(tile_heads, BLOCK, keys_len), -1e30
                ).reshape(rows, keys_len)
            old_max = max_ref[span, :]
            new_max = jnp.maximum(old_max, jnp.max(scores, axis=1, keepdims=True))
            decay = jnp.exp2((old_max - new_max) * factor)
            lane_sum = sum_ref[span, :] * decay
            weights = []
            for column in range(keys_len // DH):
                piece = jnp.exp2((scores[:, column * DH : (column + 1) * DH] - new_max) * factor)
                lane_sum = lane_sum + piece
                weights.append(piece.astype(BF16))
            sum_ref[span, :] = lane_sum
            max_ref[span, :] = new_max
            added = jnp.dot(jnp.concatenate(weights, axis=1), vals, preferred_element_type=F32)
            acc_ref[span, :] = acc_ref[span, :] * decay + added

    @pl.when(chunk == diagonal)
    def _():
        update(True)
        for head in range(heads):
            span = pl.ds(head * BLOCK, BLOCK)
            total = jnp.sum(sum_ref[span, :], axis=1, keepdims=True)
            out_ref[0, :, pl.ds(head * DH, DH)] = (acc_ref[span, :] / total).astype(BF16)

    @pl.when(chunk != diagonal)
    def _():
        update(False)


def attend(meta, q_pair, gathered, tile_heads=2):
    rows, width = q_pair.shape[1:]
    heads = width // DH
    steps = BLOCKS // CHUNK_BLOCKS + 1
    low = CHUNK_BLOCKS // 4

    def place(step, meta_ref):
        first_steps = meta_ref[2]
        second = (step >= first_steps).astype(jnp.int32)
        chunk = step - second * first_steps
        return second, chunk

    def pair_map(step, meta_ref):
        return place(step, meta_ref)[0], 0, 0

    def key_map(column):
        def index(step, meta_ref):
            chunk = place(step, meta_ref)[1]
            if low == 2:
                return chunk // 8, (chunk // 2) % 4, 0, chunk % 2, 0, column + meta_ref[3]
            zh, y, c, zl = chunk // 16, (chunk // 4) % 4, (chunk // 2) % 2, chunk % 2
            return zh * 2 + zl, y, 0, c, 0, column + meta_ref[3]

        return index

    block = (low, 1, 4, 1, BLOCK, DH)
    return pl.pallas_call(
        functools.partial(attend_kernel, heads=heads, tile_heads=tile_heads),
        grid_spec=pltpu.PrefetchScalarGridSpec(
            num_scalar_prefetch=1,
            grid=(steps,),
            in_specs=[
                pl.BlockSpec((1, rows, width), pair_map),
                pl.BlockSpec(block, key_map(0)),
                pl.BlockSpec(block, key_map(2)),
            ],
            out_specs=pl.BlockSpec((1, rows, width), pair_map),
            scratch_shapes=[pltpu.VMEM((heads * rows, DH), F32)] * 3,
        ),
        out_shape=jax.ShapeDtypeStruct((2, rows, width), BF16),
        compiler_params=params("arbitrary"),
        name="attend",
    )(meta, q_pair, gathered, gathered)


def slots_of(ids_ref):
    shape = (BLOCK, BLOCK)
    expert = lax.broadcasted_iota(jnp.int32, shape, 0)
    named = jnp.zeros(shape, F32)
    for k in range(TOP):
        named = named + jnp.where(ids_ref[k : k + 1, :] == expert, 1.0, 0.0)
    earlier = jnp.where(
        lax.broadcasted_iota(jnp.int32, shape, 0) < lax.broadcasted_iota(jnp.int32, shape, 1),
        1.0,
        0.0,
    )
    counts = jnp.dot(named.astype(BF16), earlier.astype(BF16), preferred_element_type=F32)
    return named, jnp.where(named > 0.0, counts, -1.0)


def project_kernel(
    core_ref, own_ref, got_ref, w_ref, hidden_ref, gain_ref, router_ref, ids_ref,
    h1_ref, slot_ref, route_ref, send_ref, over_ref, acc_ref,
):
    step = pl.program_id(0)
    depth = w_ref.shape[0]
    half_steps = pl.num_programs(0) // 2

    @pl.when(step == 0)
    def _():
        acc_ref[...] = jnp.zeros_like(acc_ref)

    column = pl.ds(pl.multiple_of(lax.rem(step, half_steps) * depth, depth), depth)

    @pl.when(step < half_steps)
    def _():
        acc_ref[...] += jnp.dot(own_ref[:, column], w_ref[...], preferred_element_type=F32)

    @pl.when(step >= half_steps)
    def _():
        acc_ref[...] += jnp.dot(got_ref[:, column], w_ref[...], preferred_element_type=F32)

    @pl.when(step == pl.num_programs(0) - 1)
    def _():
        h1 = (acc_ref[...] + hidden_ref[...].astype(F32)).astype(BF16)
        h1_ref[...] = h1
        h1_f = h1.astype(F32)
        mean = jnp.mean(h1_f * h1_f, axis=-1, keepdims=True)
        hn = (h1_f / jnp.sqrt(mean + 1e-06) * gain_ref[...]).astype(BF16)
        logits = jnp.dot(hn, router_ref[...], preferred_element_type=F32)
        named, slot = slots_of(ids_ref)
        slot_ref[...] = slot
        raised = jnp.where(named > 0.0, jnp.exp(jnp.transpose(logits)), 0.0)
        route_ref[...] = raised / jnp.sum(raised, axis=0, keepdims=True)
        wanted = lax.broadcasted_iota(jnp.int32, (BLOCK, MAIN, BLOCK), 1).astype(F32)
        pick = jnp.where(slot[:, None, :] == wanted, 1.0, 0.0).reshape(BLOCK * MAIN, BLOCK)
        send_ref[...] = jnp.dot(pick.astype(BF16), hn, preferred_element_type=F32).astype(BF16)
        last = jnp.where(slot == float(MAIN), 1.0, 0.0).astype(BF16)
        over_ref[...] = jnp.dot(last, hn, preferred_element_type=F32).astype(BF16)


def project(core, own, got, w_out, hidden, gain, w_router, ids_t):
    rows, half = own.shape
    width = hidden.shape[1]
    depth = 512
    half_steps = half // depth

    def w_map(step, core_ref):
        which = jnp.where(step < half_steps, core_ref[0], 1 - core_ref[0])
        return which * half_steps + lax.rem(step, half_steps), 0

    def full(shape):
        return pl.BlockSpec(shape, lambda step, core_ref: (0,) * len(shape))

    experts = w_router.shape[1]
    return pl.pallas_call(
        project_kernel,
        grid_spec=pltpu.PrefetchScalarGridSpec(
            num_scalar_prefetch=1,
            grid=(2 * half_steps,),
            in_specs=[
                full((rows, half)),
                full((rows, half)),
                pl.BlockSpec((depth, width), w_map),
                full((rows, width)),
                full((1, width)),
                full((width, experts)),
                full((TOP, rows)),
            ],
            out_specs=[
                full((rows, width)),
                full((experts, rows)),
                full((experts, rows)),
                full((experts * MAIN, width)),
                full((experts, width)),
            ],
            scratch_shapes=[pltpu.VMEM((rows, width), F32)],
        ),
        out_shape=[
            jax.ShapeDtypeStruct((rows, width), BF16),
            jax.ShapeDtypeStruct((experts, rows), F32),
            jax.ShapeDtypeStruct((experts, rows), F32),
            jax.ShapeDtypeStruct((experts * MAIN, width), BF16),
            jax.ShapeDtypeStruct((experts, width), BF16),
        ],
        compiler_params=params("arbitrary"),
        name="project",
    )(core, own, got, w_out, hidden, gain, w_router, ids_t)


def expert_kernel(
    main_ref, over_ref, gate_ref, up_ref, down_ref, y_main_ref, y_over_ref, act_ref, *, up_steps
):
    step = pl.program_id(0)
    tile = gate_ref.shape[1]
    main_rows = main_ref.shape[0]
    half = main_rows // 2
    spans = [(main_ref, y_main_ref, 0, half, 0), (main_ref, y_main_ref, half, half, half)]
    spans.append((over_ref, y_over_ref, 0, over_ref.shape[0], main_rows))

    for index in range(up_steps):

        @pl.when(step == index)
        def _(index=index):
            for source, _, start, size, place in spans:
                rows = source[start : start + size, :]
                gate = jnp.dot(rows, gate_ref[...], preferred_element_type=F32)
                up = jnp.dot(rows, up_ref[...], preferred_element_type=F32)
                act = gate / (1.0 + jnp.exp(-gate)) * up
                act_ref[place : place + size, index * tile : (index + 1) * tile] = act.astype(BF16)

    @pl.when(step >= up_steps)
    def _():
        for _, target, start, size, place in spans:
            target[start : start + size, :] = jnp.dot(
                act_ref[place : place + size, :], down_ref[...], preferred_element_type=F32
            ).astype(BF16)


def experts_of(main, over, w_gate, w_up, w_down):
    main_rows, width = main.shape
    over_rows = over.shape[0]
    hidden_units = w_gate.shape[1]
    tile = 256
    columns = 512
    up_steps = hidden_units // tile
    steps = up_steps + width // columns

    def up_map(step):
        return 0, jnp.minimum(step, up_steps - 1)

    def down_map(step):
        return 0, jnp.maximum(step - up_steps, 0)

    return pl.pallas_call(
        functools.partial(expert_kernel, up_steps=up_steps),
        grid=(steps,),
        in_specs=[
            pl.BlockSpec((main_rows, width), lambda step: (0, 0)),
            pl.BlockSpec((over_rows, width), lambda step: (0, 0)),
            pl.BlockSpec((width, tile), up_map),
            pl.BlockSpec((width, tile), up_map),
            pl.BlockSpec((hidden_units, columns), down_map),
        ],
        out_specs=[
            pl.BlockSpec((main_rows, columns), down_map),
            pl.BlockSpec((over_rows, columns), down_map),
        ],
        out_shape=[
            jax.ShapeDtypeStruct((main_rows, width), BF16),
            jax.ShapeDtypeStruct((over_rows, width), BF16),
        ],
        scratch_shapes=[pltpu.VMEM((main_rows + over_rows, hidden_units), BF16)],
        compiler_params=params("arbitrary"),
        name="experts_of",
    )(main, over, w_gate, w_up, w_down)


def combine_kernel(slot_ref, route_ref, main_ref, over_ref, h1_ref, out_ref, mix_ref, last_ref):
    @pl.when(pl.program_id(0) == 0)
    def _():
        slot = slot_ref[...]
        route = route_ref[...]
        wanted = lax.broadcasted_iota(jnp.int32, (BLOCK, MAIN, BLOCK), 1).astype(F32)
        mix = jnp.where(slot[:, None, :] == wanted, route[:, None, :], 0.0)
        mix_ref[...] = mix.reshape(BLOCK * MAIN, BLOCK).astype(BF16)
        last_ref[...] = jnp.where(slot == float(MAIN), route, 0.0).astype(BF16)

    def mixed(weights, rows):
        return lax.dot_general(
            weights, rows, (((0,), (0,)), ((), ())), preferred_element_type=F32
        )

    total = mixed(mix_ref[...], main_ref[...]) + mixed(last_ref[...], over_ref[...])
    out_ref[...] = (total + h1_ref[...].astype(F32)).astype(BF16)


def combine(slot, route, main, over, h1):
    rows, width = h1.shape
    columns = 512

    def whole(shape):
        return pl.BlockSpec(shape, lambda step: (0, 0))

    def tiled(count):
        return pl.BlockSpec((count, columns), lambda step: (0, step))

    return pl.pallas_call(
        combine_kernel,
        grid=(width // columns,),
        in_specs=[
            whole(slot.shape),
            whole(route.shape),
            tiled(main.shape[0]),
            tiled(over.shape[0]),
            tiled(rows),
        ],
        out_specs=tiled(rows),
        out_shape=jax.ShapeDtypeStruct((rows, width), BF16),
        scratch_shapes=[
            pltpu.VMEM((main.shape[0], rows), BF16),
            pltpu.VMEM((over.shape[0], rows), BF16),
        ],
        compiler_params=params("arbitrary"),
        name="combine",
    )(slot, route, main, over, h1)


def exchange(main, over):
    experts = over.shape[0]
    width = over.shape[1]
    swap = functools.partial(
        lax.all_to_all, axis_name=AXES, split_axis=0, concat_axis=0, tiled=True
    )
    main = swap(main.reshape(experts, MAIN, width)).reshape(experts * MAIN, width)
    over = swap(over.reshape(experts, width // DH, DH)).reshape(experts, width)
    return main, over


def local(
    hidden, queries, keys, values, w_out, norm_gain, w_router, expert_ids, w_gate, w_up, w_down
):
    rows = hidden.shape[0]
    device = lax.axis_index(AXES)
    core = lax.axis_index("c")
    positions = device * rows + jnp.arange(rows, dtype=jnp.int32)
    cos_t, sin_t = yarn_tables(positions, DH)
    core_arr = core.reshape(1).astype(jnp.int32)
    keep, give, kv = rotate_all(core_arr, queries, keys, values, cos_t, sin_t)
    gathered = lax.all_gather(kv, TORUS, axis=0, tiled=True)
    gathered = gathered.reshape(4, 4, 4, 2, BLOCK, 4 * DH)
    mirror = [(i, BLOCKS - 1 - i) for i in range(BLOCKS)]
    taken = lax.ppermute(give, AXES, mirror)
    other = BLOCKS - 1 - device
    meta = jnp.stack([other, device, other // CHUNK_BLOCKS + 1, core]).astype(jnp.int32)
    attn = attend(meta, jnp.stack([taken, keep]), gathered)
    got = lax.ppermute(attn[0], AXES, mirror)
    h1, slot, route, send, over = project(
        core_arr, attn[1], got, w_out, hidden, norm_gain[None, :], w_router, expert_ids.T
    )
    main, over = exchange(send, over)
    y_main, y_over = experts_of(main, over, w_gate[0], w_up[0], w_down[0])
    y_main, y_over = exchange(y_main, y_over)
    return combine(slot, route, y_main, y_over, h1)


def solution(mesh):
    torus = Mesh(mesh.devices.reshape(2, 4, 2, 2, 4), AXES)
    split = P(AXES, None)
    experts = P(AXES, None, None)
    in_specs = (
        split, split, split, split, P(), P(), P(), split, experts, experts, experts,
    )
    return jax.shard_map(
        local, mesh=torus, in_specs=in_specs, out_specs=split, check_vma=False
    )
```

```python
import functools
import math

import jax
import jax.numpy as jnp
from jax import lax
from jax.experimental import pallas as pl
from jax.experimental.pallas import tpu as pltpu
from jax.sharding import Mesh, PartitionSpec as P

DH = 128
TOP = 8
CAP = 9
MAIN = 8
BLOCK = 128
BLOCKS = 128
CHUNK_BLOCKS = 8
TILE_HEADS = 4
AXES = ("zh", "y", "c", "zl", "x")
TORUS = ("zh", "zl", "y", "x", "c")

rope_base = 1000000.0
yarn_factor = 4.0
orig_len = 32768.0
beta_fast = 32.0
beta_slow = 1.0
mscale_yarn = 0.1 * math.log(4.0) + 1.0

F32 = jnp.float32
BF16 = jnp.bfloat16
VMEM_LIMIT = 60 * 1024 * 1024


def params(*semantics):
    return pltpu.CompilerParams(
        dimension_semantics=semantics, vmem_limit_bytes=VMEM_LIMIT
    )


def yarn_tables(positions, head_size):
    half_size = head_size // 2
    index_f = jnp.arange(half_size, dtype=jnp.float32)
    pos_freq = rope_base ** (2.0 * index_f / head_size)
    inv_extra = 1.0 / pos_freq
    inv_inter = 1.0 / (yarn_factor * pos_freq)
    low_dim = max(
        math.floor(
            head_size
            * math.log(orig_len / (beta_fast * 2.0 * math.pi))
            / (2.0 * math.log(rope_base))
        ),
        0,
    )
    high_dim = min(
        math.ceil(
            head_size
            * math.log(orig_len / (beta_slow * 2.0 * math.pi))
            / (2.0 * math.log(rope_base))
        ),
        head_size - 1,
    )
    ramp_part = jnp.clip((index_f - low_dim) / max(high_dim - low_dim, 0.001), 0.0, 1.0)
    extra_part = 1.0 - ramp_part
    inverse = inv_inter * (1.0 - extra_part) + inv_extra * extra_part
    angles = positions.astype(jnp.float32)[:, None] * inverse[None, :]
    cos_half = jnp.cos(angles) * mscale_yarn
    sin_half = jnp.sin(angles) * mscale_yarn
    return (
        jnp.concatenate([cos_half, cos_half], axis=-1),
        jnp.concatenate([-sin_half, sin_half], axis=-1),
    )


def rotate_kernel(core_ref, q_ref, k_ref, v_ref, cos_ref, sin_ref, keep_ref, give_ref, kv_ref):
    core = core_ref[0]
    cos_t = cos_ref[...]
    sin_t = sin_ref[...]

    def rotated(part):
        value = part.astype(F32)
        return (value * cos_t + pltpu.roll(value, DH // 2, 1) * sin_t).astype(BF16)

    for head in range(2):
        columns = pl.ds(head * DH, DH)
        kv_ref[:, columns] = rotated(k_ref[:, columns])
    kv_ref[:, pl.ds(2 * DH, 2 * DH)] = v_ref[...]
    half = keep_ref.shape[1]
    for out_ref, which in ((keep_ref, core), (give_ref, 1 - core)):
        for head in range(half // DH):
            source = pl.ds(pl.multiple_of(which * half + head * DH, DH), DH)
            out_ref[:, pl.ds(head * DH, DH)] = rotated(q_ref[:, source])


def rotate_all(core, queries, keys, values, cos_t, sin_t):
    rows, width = queries.shape
    vmem = pl.BlockSpec(memory_space=pltpu.VMEM)
    return pl.pallas_call(
        rotate_kernel,
        in_specs=[pl.BlockSpec(memory_space=pltpu.SMEM)] + [vmem] * 5,
        out_specs=[vmem] * 3,
        out_shape=[
            jax.ShapeDtypeStruct((rows, width // 2), BF16),
            jax.ShapeDtypeStruct((rows, width // 2), BF16),
            jax.ShapeDtypeStruct((rows, 4 * DH), BF16),
        ],
        compiler_params=params(),
        name="rotate_all",
    )(core, queries, keys, values, cos_t, sin_t)


def attend_kernel(
    meta_ref, theirs_ref, own_ref, k_ref, v_ref, theirs_out_ref, own_out_ref,
    q_ref, max_ref, sum_ref, acc_ref, *, heads, tile_heads
):
    step = pl.program_id(0)
    second = step >= meta_ref[2]
    chunk = jnp.where(second, step - meta_ref[2], step)
    block = jnp.where(second, meta_ref[1], meta_ref[0])
    diagonal = block // CHUNK_BLOCKS
    keys_len = CHUNK_BLOCKS * BLOCK
    factor = math.log2(math.e) / math.sqrt(DH)
    rows = tile_heads * BLOCK
    parts = heads // tile_heads

    @pl.when(chunk == 0)
    def _():
        max_ref[...] = jnp.full_like(max_ref, -1e30)
        sum_ref[...] = jnp.zeros_like(sum_ref)
        acc_ref[...] = jnp.zeros_like(acc_ref)

    @pl.when(step == 0)
    def _():
        q_ref[...] = theirs_ref[...]

    @pl.when(step == meta_ref[2])
    def _():
        q_ref[...] = own_ref[...]

    def update(masked):
        keys = k_ref[...].reshape(keys_len, DH)
        vals = v_ref[...].reshape(keys_len, DH)
        if masked:
            offset = (block - chunk * CHUNK_BLOCKS) * BLOCK
            row_token = lax.broadcasted_iota(jnp.int32, (BLOCK, keys_len), 0) + offset
            key_token = lax.broadcasted_iota(jnp.int32, (BLOCK, keys_len), 1)
            allowed = key_token <= row_token

        def scores_of(part):
            query = jnp.concatenate(
                [q_ref[:, pl.ds((part * tile_heads + h) * DH, DH)] for h in range(tile_heads)],
                axis=0,
            )
            scores = lax.dot_general(
                query, keys, (((1,), (1,)), ((), ())), preferred_element_type=F32
            )
            if masked:
                scores = jnp.where(
                    allowed[None], scores.reshape(tile_heads, BLOCK, keys_len), -1e30
                ).reshape(rows, keys_len)
            return scores

        def absorb(part, scores):
            span = pl.ds(part * rows, rows)
            old_max = max_ref[span, :]
            new_max = jnp.maximum(old_max, jnp.max(scores, axis=1, keepdims=True))
            decay = jnp.exp2((old_max - new_max) * factor)
            lane_sum = sum_ref[span, :] * decay
            weights = []
            for column in range(keys_len // DH):
                piece = jnp.exp2((scores[:, column * DH : (column + 1) * DH] - new_max) * factor)
                lane_sum = lane_sum + piece
                weights.append(piece.astype(BF16))
            sum_ref[span, :] = lane_sum
            max_ref[span, :] = new_max
            added = jnp.dot(jnp.concatenate(weights, axis=1), vals, preferred_element_type=F32)
            acc_ref[span, :] = acc_ref[span, :] * decay + added

        scores = scores_of(0)
        for part in range(parts):
            later = scores_of(part + 1) if part + 1 < parts else None
            absorb(part, scores)
            scores = later

    @pl.when(chunk == diagonal)
    def _():
        update(True)

        def store(out_ref):
            for head in range(heads):
                span = pl.ds(head * BLOCK, BLOCK)
                total = jnp.sum(sum_ref[span, :], axis=1, keepdims=True)
                out_ref[:, pl.ds(head * DH, DH)] = (acc_ref[span, :] / total).astype(BF16)

        pl.when(second)(lambda: store(own_out_ref))
        pl.when(jnp.logical_not(second))(lambda: store(theirs_out_ref))

    @pl.when(chunk != diagonal)
    def _():
        update(False)


def attend(meta, theirs, own, gathered, tile_heads=TILE_HEADS):
    rows, width = own.shape
    heads = width // DH
    steps = BLOCKS // CHUNK_BLOCKS + 1

    def key_map(column):
        def index(step, meta_ref):
            chunk = jnp.where(step >= meta_ref[2], step - meta_ref[2], step)
            return chunk // 8, (chunk // 2) % 4, 0, chunk % 2, 0, 2 * column + meta_ref[3]

        return index

    def whole(step, meta_ref):
        return 0, 0

    piece = (2, 1, 4, 1, BLOCK, DH)
    return pl.pallas_call(
        functools.partial(attend_kernel, heads=heads, tile_heads=tile_heads),
        grid_spec=pltpu.PrefetchScalarGridSpec(
            num_scalar_prefetch=1,
            grid=(steps,),
            in_specs=[
                pl.BlockSpec((rows, width), whole),
                pl.BlockSpec((rows, width), whole),
                pl.BlockSpec(piece, key_map(0)),
                pl.BlockSpec(piece, key_map(1)),
            ],
            out_specs=[pl.BlockSpec((rows, width), whole)] * 2,
            scratch_shapes=[pltpu.VMEM((rows, width), BF16)]
            + [pltpu.VMEM((heads * rows, DH), F32)] * 3,
        ),
        out_shape=[jax.ShapeDtypeStruct((rows, width), BF16)] * 2,
        compiler_params=params("arbitrary"),
        name="attend",
    )(meta, theirs, own, gathered, gathered)


def slots_of(ids_ref):
    shape = (BLOCK, BLOCK)
    expert = lax.broadcasted_iota(jnp.int32, shape, 0)
    named = jnp.zeros(shape, F32)
    for k in range(TOP):
        named = named + jnp.where(ids_ref[k : k + 1, :] == expert, 1.0, 0.0)
    earlier = jnp.where(
        lax.broadcasted_iota(jnp.int32, shape, 0) < lax.broadcasted_iota(jnp.int32, shape, 1),
        1.0,
        0.0,
    )
    counts = jnp.dot(named.astype(BF16), earlier.astype(BF16), preferred_element_type=F32)
    return named, jnp.where(named > 0.0, counts, -1.0)


def own_kernel(core_ref, own_ref, w_ref, out_ref):
    @pl.when(pl.program_id(0) == 0)
    def _():
        out_ref[...] = jnp.zeros_like(out_ref)

    depth = w_ref.shape[0]
    column = pl.ds(pl.multiple_of(pl.program_id(0) * depth, depth), depth)
    out_ref[...] += jnp.dot(own_ref[:, column], w_ref[...], preferred_element_type=F32)


def project_own(core, own, w_out, depth=512):
    rows, half = own.shape
    width = w_out.shape[1]
    steps = half // depth
    return pl.pallas_call(
        own_kernel,
        grid_spec=pltpu.PrefetchScalarGridSpec(
            num_scalar_prefetch=1,
            grid=(steps,),
            in_specs=[
                pl.BlockSpec((rows, half), lambda step, core_ref: (0, 0)),
                pl.BlockSpec((depth, width), lambda step, core_ref: (core_ref[0] * steps + step, 0)),
            ],
            out_specs=pl.BlockSpec((rows, width), lambda step, core_ref: (0, 0)),
        ),
        out_shape=jax.ShapeDtypeStruct((rows, width), F32),
        compiler_params=params("arbitrary"),
        cost_estimate=pl.CostEstimate(
            flops=2 * rows * half * width, bytes_accessed=2 * half * width, transcendentals=0
        ),
        name="project_own",
    )(core, own, w_out)


def project_kernel(
    core_ref, part_ref, got_ref, w_ref, hidden_ref, gain_ref, router_ref, ids_ref,
    h1_ref, slot_ref, route_ref, send_ref, acc_ref, over_ref,
):
    step = pl.program_id(0)
    depth = w_ref.shape[0]

    @pl.when(step == 0)
    def _():
        acc_ref[...] = part_ref[...] + hidden_ref[...].astype(F32)

    column = pl.ds(pl.multiple_of(step * depth, depth), depth)
    acc_ref[...] += jnp.dot(got_ref[:, column], w_ref[...], preferred_element_type=F32)

    @pl.when(step == pl.num_programs(0) - 1)
    def _():
        h1 = acc_ref[...].astype(BF16)
        h1_ref[...] = h1
        h1_f = h1.astype(F32)
        mean = jnp.mean(h1_f * h1_f, axis=-1, keepdims=True)
        hn = (h1_f / jnp.sqrt(mean + 1e-06) * gain_ref[...]).astype(BF16)
        logits = jnp.dot(hn, router_ref[...], preferred_element_type=F32)
        named, slot = slots_of(ids_ref)
        slot_ref[...] = slot
        raised = jnp.where(named > 0.0, jnp.exp(jnp.transpose(logits)), 0.0)
        route_ref[...] = raised / jnp.sum(raised, axis=0, keepdims=True)
        wanted = lax.broadcasted_iota(jnp.int32, (BLOCK, MAIN, BLOCK), 1).astype(F32)
        pick = jnp.where(slot[:, None, :] == wanted, 1.0, 0.0).reshape(BLOCK * MAIN, BLOCK)
        pick = pick.astype(BF16)
        last = jnp.where(slot == float(MAIN), 1.0, 0.0).astype(BF16)
        tiles = hn.shape[1] // DH
        for tile in range(tiles):
            part = hn[:, tile * DH : (tile + 1) * DH]
            rows = jnp.dot(pick, part, preferred_element_type=F32)
            send_ref[:, tile * MAIN : (tile + 1) * MAIN, :] = rows.reshape(
                BLOCK, MAIN, DH
            ).astype(BF16)
            over_ref[:, tile, :] = jnp.dot(last, part, preferred_element_type=F32)
        send_ref[:, tiles * MAIN :, :] = over_ref[...].astype(BF16)


def project(core, part, got, w_out, hidden, gain, w_router, ids_t, depth=512):
    rows, half = got.shape
    width = hidden.shape[1]
    steps = half // depth

    def full(shape):
        return pl.BlockSpec(shape, lambda step, core_ref: (0,) * len(shape))

    experts = w_router.shape[1]
    packed = (experts, CAP * width // DH, DH)
    return pl.pallas_call(
        project_kernel,
        grid_spec=pltpu.PrefetchScalarGridSpec(
            num_scalar_prefetch=1,
            grid=(steps,),
            in_specs=[
                full((rows, width)),
                full((rows, half)),
                pl.BlockSpec(
                    (depth, width), lambda step, core_ref: ((1 - core_ref[0]) * steps + step, 0)
                ),
                full((rows, width)),
                full((1, width)),
                full((width, experts)),
                full((TOP, rows)),
            ],
            out_specs=[
                full((rows, width)),
                full((experts, rows)),
                full((experts, rows)),
                full(packed),
            ],
            scratch_shapes=[
                pltpu.VMEM((rows, width), F32),
                pltpu.VMEM((experts, width // DH, DH), F32),
            ],
        ),
        out_shape=[
            jax.ShapeDtypeStruct((rows, width), BF16),
            jax.ShapeDtypeStruct((experts, rows), F32),
            jax.ShapeDtypeStruct((experts, rows), F32),
            jax.ShapeDtypeStruct(packed, BF16),
        ],
        compiler_params=params("arbitrary"),
        name="project",
    )(core, part, got, w_out, hidden, gain, w_router, ids_t)


def expert_kernel(in_ref, gate_ref, up_ref, down_ref, out_ref, rows_ref, act_ref, over_ref, *, up_steps):
    step = pl.program_id(0)
    tile = gate_ref.shape[1]
    sources = in_ref.shape[0]
    main_rows = sources * MAIN
    width = gate_ref.shape[0]
    tiles = width // DH

    @pl.when(step == 0)
    def _():
        over_ref[...] = in_ref[:, tiles * MAIN :, :].astype(F32)
        for place in range(tiles):
            columns = pl.ds(place * DH, DH)
            rows_ref[:main_rows, columns] = in_ref[:, place * MAIN : (place + 1) * MAIN, :].reshape(
                main_rows, DH
            )
            rows_ref[main_rows:, columns] = over_ref[:, place, :].astype(BF16)

    half = main_rows // 2
    spans = [(0, half), (half, half), (main_rows, sources)]
    for index in range(up_steps):

        @pl.when(step == index)
        def _(index=index):
            for start, size in spans:
                rows = rows_ref[start : start + size, :]
                gate = jnp.dot(rows, gate_ref[...], preferred_element_type=F32)
                up = jnp.dot(rows, up_ref[...], preferred_element_type=F32)
                act = gate / (1.0 + jnp.exp(-gate)) * up
                act_ref[start : start + size, index * tile : (index + 1) * tile] = act.astype(BF16)

    columns = down_ref.shape[1]
    for index in range(width // columns):

        @pl.when(step == up_steps + index)
        def _(index=index):
            first = index * columns // DH
            for start, size in spans:
                rows = jnp.dot(
                    act_ref[start : start + size, :], down_ref[...], preferred_element_type=F32
                )
                for place in range(columns // DH):
                    piece = rows[:, place * DH : (place + 1) * DH]
                    if start < main_rows:
                        some = pl.ds(start // MAIN, size // MAIN)
                        out_ref[some, (first + place) * MAIN : (first + place + 1) * MAIN, :] = (
                            piece.reshape(size // MAIN, MAIN, DH).astype(BF16)
                        )
                    else:
                        over_ref[:, first + place, :] = piece
            if index == width // columns - 1:
                out_ref[:, tiles * MAIN :, :] = over_ref[...].astype(BF16)


def experts_of(packed, w_gate, w_up, w_down):
    sources = packed.shape[0]
    width, hidden_units = w_gate.shape
    tile = 256
    columns = 512
    up_steps = hidden_units // tile
    steps = up_steps + width // columns
    rows = sources * CAP

    def up_map(step):
        return 0, jnp.minimum(step, up_steps - 1)

    def down_map(step):
        return 0, jnp.maximum(step - up_steps, 0)

    def whole(step):
        return 0, 0, 0

    return pl.pallas_call(
        functools.partial(expert_kernel, up_steps=up_steps),
        grid=(steps,),
        in_specs=[
            pl.BlockSpec(packed.shape, whole),
            pl.BlockSpec((width, tile), up_map),
            pl.BlockSpec((width, tile), up_map),
            pl.BlockSpec((hidden_units, columns), down_map),
        ],
        out_specs=pl.BlockSpec(packed.shape, whole),
        out_shape=jax.ShapeDtypeStruct(packed.shape, BF16),
        scratch_shapes=[
            pltpu.VMEM((rows, width), BF16),
            pltpu.VMEM((rows, hidden_units), BF16),
            pltpu.VMEM((sources, width // DH, DH), F32),
        ],
        compiler_params=params("arbitrary"),
        name="experts_of",
    )(packed, w_gate, w_up, w_down)


def combine_kernel(slot_ref, route_ref, in_ref, h1_ref, out_ref, over_ref):
    slot = slot_ref[...]
    route = route_ref[...]
    wanted = lax.broadcasted_iota(jnp.int32, (BLOCK, MAIN, BLOCK), 1).astype(F32)
    mix = jnp.where(slot[:, None, :] == wanted, route[:, None, :], 0.0)
    mix = mix.reshape(BLOCK * MAIN, BLOCK).astype(BF16)
    last = jnp.where(slot == float(MAIN), route, 0.0).astype(BF16)
    tiles = h1_ref.shape[1] // DH
    over_ref[...] = in_ref[:, tiles * MAIN :, :].astype(F32)

    def mixed(weights, rows):
        return lax.dot_general(
            weights, rows, (((0,), (0,)), ((), ())), preferred_element_type=F32
        )

    per = 2
    for place in range(0, tiles, per):
        columns = pl.ds(place * DH, per * DH)
        spots = range(place, place + per)
        rows = jnp.concatenate(
            [
                in_ref[:, p * MAIN : (p + 1) * MAIN, :].reshape(BLOCK * MAIN, DH)
                for p in spots
            ],
            axis=1,
        )
        extra = jnp.concatenate([over_ref[:, p, :].astype(BF16) for p in spots], axis=1)
        total = mixed(mix, rows) + mixed(last, extra)
        out_ref[:, columns] = (total + h1_ref[:, columns].astype(F32)).astype(BF16)


def combine(slot, route, packed, h1):
    vmem = pl.BlockSpec(memory_space=pltpu.VMEM)
    return pl.pallas_call(
        combine_kernel,
        in_specs=[vmem] * 4,
        out_specs=vmem,
        out_shape=jax.ShapeDtypeStruct(h1.shape, BF16),
        scratch_shapes=[pltpu.VMEM((packed.shape[0], h1.shape[1] // DH, DH), F32)],
        compiler_params=params(),
        name="combine",
    )(slot, route, packed, h1)


def exchange(packed):
    return lax.all_to_all(packed, AXES, split_axis=0, concat_axis=0, tiled=True)


def local(
    hidden, queries, keys, values, w_out, norm_gain, w_router, expert_ids, w_gate, w_up, w_down
):
    rows = hidden.shape[0]
    device = lax.axis_index(AXES)
    core = lax.axis_index("c")
    positions = device * rows + jnp.arange(rows, dtype=jnp.int32)
    cos_t, sin_t = yarn_tables(positions, DH)
    core_arr = core.reshape(1).astype(jnp.int32)
    keep, give, kv = rotate_all(core_arr, queries, keys, values, cos_t, sin_t)
    gathered = lax.all_gather(kv, TORUS, axis=0, tiled=True)
    gathered = gathered.reshape(4, 4, 4, 2, BLOCK, 4 * DH)
    mirror = [(i, BLOCKS - 1 - i) for i in range(BLOCKS)]
    taken = lax.ppermute(give, AXES, mirror)
    other = BLOCKS - 1 - device
    meta = jnp.stack([other, device, other // CHUNK_BLOCKS + 1, core]).astype(jnp.int32)
    theirs, own = attend(meta, taken, keep, gathered)
    got = lax.ppermute(theirs, AXES, mirror)
    part = project_own(core_arr, own, w_out)
    h1, slot, route, send = project(
        core_arr, part, got, w_out, hidden, norm_gain[None, :], w_router, expert_ids.T
    )
    returned = exchange(experts_of(exchange(send), w_gate[0], w_up[0], w_down[0]))
    return combine(slot, route, returned, h1)


def solution(mesh):
    torus = Mesh(mesh.devices.reshape(2, 4, 2, 2, 4), AXES)
    split = P(AXES, None)
    experts = P(AXES, None, None)
    in_specs = (
        split, split, split, split, P(), P(), P(), split, experts, experts, experts,
    )
    return jax.shard_map(
        local, mesh=torus, in_specs=in_specs, out_specs=split, check_vma=False
    )
```

```python
import functools
import math

import jax
import jax.numpy as jnp
from jax import lax
from jax.experimental import pallas as pl
from jax.experimental.pallas import tpu as pltpu
from jax.sharding import Mesh, PartitionSpec as P


DH = 128
TOP = 8
CAP = 9
MAIN = 8
BLOCK = 128
BLOCKS = 128
UNIT = 4
FAR = 1 << 20
TILE_HEADS = 4
AXES = ("zh", "y", "c", "zl", "x")
RING_Z = ("zh", "zl")
RING_Y = ("y",)
OFFSETS = (0, -1, 1, 2)

rope_base = 1000000.0
yarn_factor = 4.0
orig_len = 32768.0
beta_fast = 32.0
beta_slow = 1.0
mscale_yarn = 0.1 * math.log(4.0) + 1.0


F32 = jnp.float32
BF16 = jnp.bfloat16
VMEM_LIMIT = 60 * 1024 * 1024


def params(*semantics):
    return pltpu.CompilerParams(
        dimension_semantics=semantics, vmem_limit_bytes=VMEM_LIMIT
    )


def yarn_tables(positions, head_size):
    half_size = head_size // 2
    index_f = jnp.arange(half_size, dtype=jnp.float32)
    pos_freq = rope_base ** (2.0 * index_f / head_size)
    inv_extra = 1.0 / pos_freq
    inv_inter = 1.0 / (yarn_factor * pos_freq)
    low_dim = max(
        math.floor(
            head_size
            * math.log(orig_len / (beta_fast * 2.0 * math.pi))
            / (2.0 * math.log(rope_base))
        ),
        0,
    )
    high_dim = min(
        math.ceil(
            head_size
            * math.log(orig_len / (beta_slow * 2.0 * math.pi))
            / (2.0 * math.log(rope_base))
        ),
        head_size - 1,
    )
    ramp_part = jnp.clip((index_f - low_dim) / max(high_dim - low_dim, 0.001), 0.0, 1.0)
    extra_part = 1.0 - ramp_part
    inverse = inv_inter * (1.0 - extra_part) + inv_extra * extra_part
    angles = positions.astype(jnp.float32)[:, None] * inverse[None, :]
    cos_half = jnp.cos(angles) * mscale_yarn
    sin_half = jnp.sin(angles) * mscale_yarn
    return (
        jnp.concatenate([cos_half, cos_half], axis=-1),
        jnp.concatenate([-sin_half, sin_half], axis=-1),
    )


def rotate_kernel(
    core_ref, q_ref, k_ref, v_ref, cos_ref, sin_ref, keep_ref, give_ref, keep_kv_ref, give_kv_ref
):
    core = core_ref[0]
    cos_t = cos_ref[...]
    sin_t = sin_ref[...]

    def rotated(part):
        value = part.astype(F32)
        return (value * cos_t + pltpu.roll(value, DH // 2, 1) * sin_t).astype(BF16)

    half = keep_ref.shape[1]
    for q_out, kv_out, which in (
        (keep_ref, keep_kv_ref, core),
        (give_ref, give_kv_ref, 1 - core),
    ):
        head_span = pl.ds(pl.multiple_of(which * DH, DH), DH)
        kv_out[:, :DH] = rotated(k_ref[:, head_span])
        kv_out[:, DH:] = v_ref[:, head_span]
        for head in range(half // DH):
            source = pl.ds(pl.multiple_of(which * half + head * DH, DH), DH)
            q_out[:, pl.ds(head * DH, DH)] = rotated(q_ref[:, source])


def rotate_all(core, queries, keys, values, cos_t, sin_t):
    rows, width = queries.shape
    vmem = pl.BlockSpec(memory_space=pltpu.VMEM)
    return pl.pallas_call(
        rotate_kernel,
        in_specs=[pl.BlockSpec(memory_space=pltpu.SMEM)] + [vmem] * 5,
        out_specs=[vmem] * 4,
        out_shape=[jax.ShapeDtypeStruct((rows, width // 2), BF16)] * 2
        + [jax.ShapeDtypeStruct((rows, 2 * DH), BF16)] * 2,
        compiler_params=params(),
        name="rotate_all",
    )(core, queries, keys, values, cos_t, sin_t)


def first_block(z, y, c):
    return z // 2 * 64 + y * 16 + c * 8 + z % 2 * 4


def attend_kernel(meta_ref, theirs_ref, own_ref, *refs, units, pieces, heads, tile_heads, first, last):
    piece_refs, refs = refs[:pieces], refs[pieces:]
    if not first:
        state_in, refs = refs[:3], refs[3:]
    if last:
        out_refs, refs = refs[:2], refs[2:]
    state, refs = refs[:3], refs[3:]
    kv_ref, q_ref, base_ref, list_ref, sem_ref = refs
    unit_rows = UNIT * BLOCK
    copies = []
    place = 0
    for index, piece in enumerate(piece_refs):
        size = piece.shape[0]
        copies.append(
            pltpu.make_async_copy(piece, kv_ref.at[pl.ds(place, size), :], sem_ref.at[index])
        )
        copies[-1].start()
        place += size
    max_ref, sum_ref, acc_ref = state
    if first:
        max_ref[...] = jnp.full_like(max_ref, -1e30)
        sum_ref[...] = jnp.zeros_like(sum_ref)
        acc_ref[...] = jnp.zeros_like(acc_ref)
    else:
        for source, target in zip(state_in, state):
            target[...] = source[...]
    q_ref[0] = theirs_ref[...]
    q_ref[1] = own_ref[...]
    for index, (z_off, y_off, c) in enumerate(units):
        base_ref[index] = first_block((meta_ref[2] + z_off) % 4, (meta_ref[3] + y_off) % 4, c)
    for copy in copies:
        copy.wait()

    factor = math.log2(math.e) / math.sqrt(DH)
    rows = tile_heads * BLOCK
    parts = heads // tile_heads
    keys_len = 2 * unit_rows

    @pl.loop(0, 2)
    def _(which):
        block = meta_ref[which]

        def update(u0, u1, masked):
            starts = [pl.multiple_of(jnp.maximum(u, 0) * unit_rows, unit_rows) for u in (u0, u1)]
            keys = jnp.concatenate([kv_ref[pl.ds(s, unit_rows), :DH] for s in starts], axis=0)
            vals = jnp.concatenate([kv_ref[pl.ds(s, unit_rows), DH:] for s in starts], axis=0)
            if masked:
                bases = [jnp.where(u < 0, FAR, base_ref[jnp.maximum(u, 0)]) for u in (u0, u1)]
                shape = (BLOCK, unit_rows)
                row_token = lax.broadcasted_iota(jnp.int32, shape, 0)
                key_token = lax.broadcasted_iota(jnp.int32, shape, 1)
                allowed = jnp.concatenate(
                    [
                        jnp.where(key_token + (base - block) * BLOCK <= row_token, 1, 0)
                        for base in bases
                    ],
                    axis=1,
                )

            def scores_of(part):
                query = jnp.concatenate(
                    [
                        q_ref[which, :, pl.ds((part * tile_heads + h) * DH, DH)]
                        for h in range(tile_heads)
                    ],
                    axis=0,
                )
                scores = lax.dot_general(
                    query, keys, (((1,), (1,)), ((), ())), preferred_element_type=F32
                )
                if masked:
                    scores = jnp.where(
                        allowed[None] > 0, scores.reshape(tile_heads, BLOCK, keys_len), -1e30
                    ).reshape(rows, keys_len)
                return scores

            def absorb(part, scores):
                start = pl.multiple_of((which * heads + part * tile_heads) * BLOCK, BLOCK)
                span = pl.ds(start, rows)
                old_max = max_ref[span, :]
                new_max = jnp.maximum(old_max, jnp.max(scores, axis=1, keepdims=True))
                decay = jnp.exp2((old_max - new_max) * factor)
                lane_sum = sum_ref[span, :] * decay
                weights = []
                for column in range(keys_len // DH):
                    some = scores[:, column * DH : (column + 1) * DH]
                    piece = jnp.exp2((some - new_max) * factor)
                    lane_sum = lane_sum + piece
                    weights.append(piece.astype(BF16))
                sum_ref[span, :] = lane_sum
                max_ref[span, :] = new_max
                added = jnp.dot(jnp.concatenate(weights, axis=1), vals, preferred_element_type=F32)
                acc_ref[span, :] = acc_ref[span, :] * decay + added

            scores = scores_of(0)
            for part in range(parts):
                later = scores_of(part + 1) if part + 1 < parts else None
                absorb(part, scores)
                scores = later

        count = jnp.int32(0)
        diagonal = jnp.int32(-1)
        for unit in range(len(units)):
            base = base_ref[unit]
            list_ref[count] = unit
            count = count + jnp.where(base + UNIT <= block, 1, 0)
            diagonal = jnp.where(
                jnp.logical_and(base <= block, block < base + UNIT), unit, diagonal
            )
        whole = count // 2

        @pl.loop(0, whole)
        def _(step):
            update(list_ref[2 * step], list_ref[2 * step + 1], False)

        odd = jnp.where(count > 2 * whole, list_ref[jnp.maximum(count - 1, 0)], -1)

        @pl.when(jnp.logical_or(odd >= 0, diagonal >= 0))
        def _():
            update(odd, diagonal, True)

    if last:
        for head in range(2 * heads):
            span = pl.ds(head * BLOCK, BLOCK)
            total = jnp.sum(sum_ref[span, :], axis=1, keepdims=True)
            out_refs[head // heads][:, pl.ds(head % heads * DH, DH)] = (
                acc_ref[span, :] / total
            ).astype(BF16)


def attend(meta, units, theirs, own, pieces, state=None, last=False, tile_heads=TILE_HEADS):
    rows, width = own.shape
    heads = width // DH
    vmem = pl.BlockSpec(memory_space=pltpu.VMEM)
    states = [(2 * heads * rows, DH)] * 3
    scratch = [
        pltpu.VMEM((len(units) * UNIT * BLOCK, 2 * DH), BF16),
        pltpu.VMEM((2, rows, width), BF16),
        pltpu.SMEM((len(units),), jnp.int32),
        pltpu.SMEM((len(units) + 1,), jnp.int32),
        pltpu.SemaphoreType.DMA((len(pieces),)),
    ]
    if last:
        scratch = [pltpu.VMEM(shape, F32) for shape in states] + scratch
        out_shape = [jax.ShapeDtypeStruct((rows, width), BF16)] * 2
    else:
        out_shape = [jax.ShapeDtypeStruct(shape, F32) for shape in states]
    state = [] if state is None else list(state)
    kernel = functools.partial(
        attend_kernel,
        units=units,
        pieces=len(pieces),
        heads=heads,
        tile_heads=tile_heads,
        first=not state,
        last=last,
    )
    keys_seen = len(units) * UNIT * BLOCK
    return pl.pallas_call(
        kernel,
        in_specs=[pl.BlockSpec(memory_space=pltpu.SMEM), vmem, vmem]
        + [pl.BlockSpec(memory_space=pl.ANY)] * len(pieces)
        + [vmem] * len(state),
        out_specs=[vmem] * len(out_shape),
        out_shape=out_shape,
        scratch_shapes=scratch,
        compiler_params=params(),
        cost_estimate=pl.CostEstimate(
            flops=4 * keys_seen * heads * rows * DH,
            bytes_accessed=keys_seen * 4 * DH,
            transcendentals=keys_seen * heads * rows,
        ),
        name="attend_last" if last else "attend_more" if state else "attend_first",
    )(meta, theirs, own, *pieces, *state)


def slots_of(ids_ref):
    shape = (BLOCK, BLOCK)
    expert = lax.broadcasted_iota(jnp.int32, shape, 0)
    named = jnp.zeros(shape, F32)
    for k in range(TOP):
        named = named + jnp.where(ids_ref[k : k + 1, :] == expert, 1.0, 0.0)
    earlier = jnp.where(
        lax.broadcasted_iota(jnp.int32, shape, 0) < lax.broadcasted_iota(jnp.int32, shape, 1),
        1.0,
        0.0,
    )
    counts = jnp.dot(named.astype(BF16), earlier.astype(BF16), preferred_element_type=F32)
    return named, jnp.where(named > 0.0, counts, -1.0)


def own_kernel(core_ref, own_ref, w_ref, out_ref):
    @pl.when(pl.program_id(0) == 0)
    def _():
        out_ref[...] = jnp.zeros_like(out_ref)

    depth = w_ref.shape[0]
    column = pl.ds(pl.multiple_of(pl.program_id(0) * depth, depth), depth)
    out_ref[...] += jnp.dot(own_ref[:, column], w_ref[...], preferred_element_type=F32)


def project_own(core, own, w_out, depth=512):
    rows, half = own.shape
    width = w_out.shape[1]
    steps = half // depth
    return pl.pallas_call(
        own_kernel,
        grid_spec=pltpu.PrefetchScalarGridSpec(
            num_scalar_prefetch=1,
            grid=(steps,),
            in_specs=[
                pl.BlockSpec((rows, half), lambda step, core_ref: (0, 0)),
                pl.BlockSpec((depth, width), lambda step, core_ref: (core_ref[0] * steps + step, 0)),
            ],
            out_specs=pl.BlockSpec((rows, width), lambda step, core_ref: (0, 0)),
        ),
        out_shape=jax.ShapeDtypeStruct((rows, width), F32),
        compiler_params=params("arbitrary"),
        cost_estimate=pl.CostEstimate(
            flops=2 * rows * half * width, bytes_accessed=2 * half * width, transcendentals=0
        ),
        name="project_own",
    )(core, own, w_out)


def project_kernel(
    core_ref, part_ref, got_ref, w_ref, hidden_ref, gain_ref, router_ref, ids_ref,
    h1_ref, slot_ref, route_ref, send_ref, acc_ref, over_ref,
):
    step = pl.program_id(0)
    depth = w_ref.shape[0]

    @pl.when(step == 0)
    def _():
        acc_ref[...] = part_ref[...] + hidden_ref[...].astype(F32)

    column = pl.ds(pl.multiple_of(step * depth, depth), depth)
    acc_ref[...] += jnp.dot(got_ref[:, column], w_ref[...], preferred_element_type=F32)

    @pl.when(step == pl.num_programs(0) - 1)
    def _():
        h1 = acc_ref[...].astype(BF16)
        h1_ref[...] = h1
        h1_f = h1.astype(F32)
        mean = jnp.mean(h1_f * h1_f, axis=-1, keepdims=True)
        hn = (h1_f / jnp.sqrt(mean + 1e-06) * gain_ref[...]).astype(BF16)
        logits = jnp.dot(hn, router_ref[...], preferred_element_type=F32)
        named, slot = slots_of(ids_ref)
        slot_ref[...] = slot
        raised = jnp.where(named > 0.0, jnp.exp(jnp.transpose(logits)), 0.0)
        route_ref[...] = raised / jnp.sum(raised, axis=0, keepdims=True)
        wanted = lax.broadcasted_iota(jnp.int32, (BLOCK, MAIN, BLOCK), 1).astype(F32)
        pick = jnp.where(slot[:, None, :] == wanted, 1.0, 0.0).reshape(BLOCK * MAIN, BLOCK)
        pick = pick.astype(BF16)
        last = jnp.where(slot == float(MAIN), 1.0, 0.0).astype(BF16)
        tiles = hn.shape[1] // DH
        for tile in range(tiles):
            part = hn[:, tile * DH : (tile + 1) * DH]
            rows = jnp.dot(pick, part, preferred_element_type=F32)
            send_ref[:, tile * MAIN : (tile + 1) * MAIN, :] = rows.reshape(
                BLOCK, MAIN, DH
            ).astype(BF16)
            over_ref[:, tile, :] = jnp.dot(last, part, preferred_element_type=F32)
        send_ref[:, tiles * MAIN :, :] = over_ref[...].astype(BF16)


def project(core, part, got, w_out, hidden, gain, w_router, ids_t, depth=512):
    rows, half = got.shape
    width = hidden.shape[1]
    steps = half // depth

    def full(shape):
        return pl.BlockSpec(shape, lambda step, core_ref: (0,) * len(shape))

    experts = w_router.shape[1]
    packed = (experts, CAP * width // DH, DH)
    return pl.pallas_call(
        project_kernel,
        grid_spec=pltpu.PrefetchScalarGridSpec(
            num_scalar_prefetch=1,
            grid=(steps,),
            in_specs=[
                full((rows, width)),
                full((rows, half)),
                pl.BlockSpec(
                    (depth, width), lambda step, core_ref: ((1 - core_ref[0]) * steps + step, 0)
                ),
                full((rows, width)),
                full((1, width)),
                full((width, experts)),
                full((TOP, rows)),
            ],
            out_specs=[
                full((rows, width)),
                full((experts, rows)),
                full((experts, rows)),
                full(packed),
            ],
            scratch_shapes=[
                pltpu.VMEM((rows, width), F32),
                pltpu.VMEM((experts, width // DH, DH), F32),
            ],
        ),
        out_shape=[
            jax.ShapeDtypeStruct((rows, width), BF16),
            jax.ShapeDtypeStruct((experts, rows), F32),
            jax.ShapeDtypeStruct((experts, rows), F32),
            jax.ShapeDtypeStruct(packed, BF16),
        ],
        compiler_params=params("arbitrary"),
        name="project",
    )(core, part, got, w_out, hidden, gain, w_router, ids_t)


def expert_kernel(in_ref, gate_ref, up_ref, down_ref, out_ref, rows_ref, act_ref, over_ref, *, up_steps):
    step = pl.program_id(0)
    tile = gate_ref.shape[1]
    sources = in_ref.shape[0]
    main_rows = sources * MAIN
    width = gate_ref.shape[0]
    tiles = width // DH

    @pl.when(step == 0)
    def _():
        over_ref[...] = in_ref[:, tiles * MAIN :, :].astype(F32)
        for place in range(tiles):
            columns = pl.ds(place * DH, DH)
            rows_ref[:main_rows, columns] = in_ref[:, place * MAIN : (place + 1) * MAIN, :].reshape(
                main_rows, DH
            )
            rows_ref[main_rows:, columns] = over_ref[:, place, :].astype(BF16)

    half = main_rows // 2
    spans = [(0, half), (half, half), (main_rows, sources)]
    for index in range(up_steps):

        @pl.when(step == index)
        def _(index=index):
            for start, size in spans:
                rows = rows_ref[start : start + size, :]
                gate = jnp.dot(rows, gate_ref[...], preferred_element_type=F32)
                up = jnp.dot(rows, up_ref[...], preferred_element_type=F32)
                act = gate / (1.0 + jnp.exp(-gate)) * up
                act_ref[start : start + size, index * tile : (index + 1) * tile] = act.astype(BF16)

    columns = down_ref.shape[1]
    for index in range(width // columns):

        @pl.when(step == up_steps + index)
        def _(index=index):
            first = index * columns // DH
            for start, size in spans:
                rows = jnp.dot(
                    act_ref[start : start + size, :], down_ref[...], preferred_element_type=F32
                )
                for place in range(columns // DH):
                    piece = rows[:, place * DH : (place + 1) * DH]
                    if start < main_rows:
                        some = pl.ds(start // MAIN, size // MAIN)
                        out_ref[some, (first + place) * MAIN : (first + place + 1) * MAIN, :] = (
                            piece.reshape(size // MAIN, MAIN, DH).astype(BF16)
                        )
                    else:
                        over_ref[:, first + place, :] = piece
            if index == width // columns - 1:
                out_ref[:, tiles * MAIN :, :] = over_ref[...].astype(BF16)


def experts_of(packed, w_gate, w_up, w_down):
    sources = packed.shape[0]
    width, hidden_units = w_gate.shape
    tile = 256
    columns = 512
    up_steps = hidden_units // tile
    steps = up_steps + width // columns
    rows = sources * CAP

    def up_map(step):
        return 0, jnp.minimum(step, up_steps - 1)

    def down_map(step):
        return 0, jnp.maximum(step - up_steps, 0)

    def whole(step):
        return 0, 0, 0

    return pl.pallas_call(
        functools.partial(expert_kernel, up_steps=up_steps),
        grid=(steps,),
        in_specs=[
            pl.BlockSpec(packed.shape, whole),
            pl.BlockSpec((width, tile), up_map),
            pl.BlockSpec((width, tile), up_map),
            pl.BlockSpec((hidden_units, columns), down_map),
        ],
        out_specs=pl.BlockSpec(packed.shape, whole),
        out_shape=jax.ShapeDtypeStruct(packed.shape, BF16),
        scratch_shapes=[
            pltpu.VMEM((rows, width), BF16),
            pltpu.VMEM((rows, hidden_units), BF16),
            pltpu.VMEM((sources, width // DH, DH), F32),
        ],
        compiler_params=params("arbitrary"),
        name="experts_of",
    )(packed, w_gate, w_up, w_down)


def combine_kernel(slot_ref, route_ref, in_ref, h1_ref, out_ref, over_ref):
    slot = slot_ref[...]
    route = route_ref[...]
    wanted = lax.broadcasted_iota(jnp.int32, (BLOCK, MAIN, BLOCK), 1).astype(F32)
    mix = jnp.where(slot[:, None, :] == wanted, route[:, None, :], 0.0)
    mix = mix.reshape(BLOCK * MAIN, BLOCK).astype(BF16)
    last = jnp.where(slot == float(MAIN), route, 0.0).astype(BF16)
    tiles = h1_ref.shape[1] // DH
    over_ref[...] = in_ref[:, tiles * MAIN :, :].astype(F32)

    def mixed(weights, rows):
        return lax.dot_general(
            weights, rows, (((0,), (0,)), ((), ())), preferred_element_type=F32
        )

    per = 2
    for place in range(0, tiles, per):
        columns = pl.ds(place * DH, per * DH)
        spots = range(place, place + per)
        rows = jnp.concatenate(
            [
                in_ref[:, p * MAIN : (p + 1) * MAIN, :].reshape(BLOCK * MAIN, DH)
                for p in spots
            ],
            axis=1,
        )
        extra = jnp.concatenate([over_ref[:, p, :].astype(BF16) for p in spots], axis=1)
        total = mixed(mix, rows) + mixed(last, extra)
        out_ref[:, columns] = (total + h1_ref[:, columns].astype(F32)).astype(BF16)


def combine(slot, route, packed, h1):
    vmem = pl.BlockSpec(memory_space=pltpu.VMEM)
    return pl.pallas_call(
        combine_kernel,
        in_specs=[vmem] * 4,
        out_specs=vmem,
        out_shape=jax.ShapeDtypeStruct(h1.shape, BF16),
        scratch_shapes=[pltpu.VMEM((packed.shape[0], h1.shape[1] // DH, DH), F32)],
        compiler_params=params(),
        name="combine",
    )(slot, route, packed, h1)


def exchange(packed):
    return lax.all_to_all(packed, AXES, split_axis=0, concat_axis=0, tiled=True)


def ring_near(piece, axes):
    left = lax.ppermute(piece, axes, [(i, (i + 1) % 4) for i in range(4)])
    right = lax.ppermute(piece, axes, [(i, (i + 3) % 4) for i in range(4)])
    return left, right


def ring_far(left, right, axes):
    half = left.shape[0] // 2
    low = lax.ppermute(left[:half], axes, [(i, (i + 1) % 4) for i in range(4)])
    high = lax.ppermute(right[half:], axes, [(i, (i + 3) % 4) for i in range(4)])
    return low, high


def ring_gather(piece, axes):
    left, right = ring_near(piece, axes)
    return jnp.concatenate([piece, left, right, *ring_far(left, right, axes)], axis=0)


def local(
    hidden, queries, keys, values, w_out, norm_gain, w_router, expert_ids, w_gate, w_up, w_down
):
    rows = hidden.shape[0]
    device = lax.axis_index(AXES)
    core = lax.axis_index("c")
    positions = device * rows + jnp.arange(rows, dtype=jnp.int32)
    cos_t, sin_t = yarn_tables(positions, DH)
    core_arr = core.reshape(1).astype(jnp.int32)
    keep, give, keep_kv, give_kv = rotate_all(core_arr, queries, keys, values, cos_t, sin_t)
    mirror = [(i, BLOCKS - 1 - i) for i in range(BLOCKS)]
    taken = lax.ppermute(give, AXES, mirror)
    other_kv = lax.ppermute(give_kv, ("c",), [(0, 1), (1, 0)])
    is_low = core == 0
    chip = jnp.concatenate(
        [jnp.where(is_low, keep_kv, other_kv), jnp.where(is_low, other_kv, keep_kv)], axis=0
    )
    row = lax.all_gather(chip, ("x",), axis=0)
    low = row[:, :rows].reshape(UNIT * rows, 2 * DH)
    high = row[:, rows:].reshape(UNIT * rows, 2 * DH)
    low = ring_gather(low, RING_Y)
    high = ring_gather(high, RING_Z)
    low_near = ring_near(low, RING_Z)
    high_near = ring_near(high, RING_Y)
    low_far = ring_far(*low_near, RING_Z)
    high_far = ring_far(*high_near, RING_Y)

    def units(order):
        return [(outer, inner, 0) for outer in order for inner in OFFSETS] + [
            (inner, outer, 1) for outer in order for inner in OFFSETS
        ]

    meta = jnp.stack(
        [BLOCKS - 1 - device, device, lax.axis_index(RING_Z), lax.axis_index(RING_Y)]
    ).astype(jnp.int32)
    state = attend(meta, units((0,)), taken, keep, [low, high])
    state = attend(meta, units((-1, 1)), taken, keep, [*low_near, *high_near], state=state)
    theirs, own = attend(
        meta, units((2,)), taken, keep, [*low_far, *high_far], state=state, last=True
    )
    got = lax.ppermute(theirs, AXES, mirror)
    part = project_own(core_arr, own, w_out)
    h1, slot, route, send = project(
        core_arr, part, got, w_out, hidden, norm_gain[None, :], w_router, expert_ids.T
    )
    returned = exchange(experts_of(exchange(send), w_gate[0], w_up[0], w_down[0]))
    return combine(slot, route, returned, h1)


def solution(mesh):
    torus = Mesh(mesh.devices.reshape(2, 4, 2, 2, 4), AXES)
    split = P(AXES, None)
    experts = P(AXES, None, None)
    in_specs = (
        split, split, split, split, P(), P(), P(), split, experts, experts, experts,
    )
    return jax.shard_map(local, mesh=torus, in_specs=in_specs, out_specs=split, check_vma=False)
```

```python
import functools
import math

import jax
import jax.numpy as jnp
from jax import lax
from jax.experimental import pallas as pl
from jax.experimental.pallas import tpu as pltpu
from jax.sharding import Mesh, PartitionSpec as P


DH = 128
TOP = 8
CAP = 9
MAIN = 8
STRIPE = 48
BLOCK = 128
BLOCKS = 128
UNIT = 4
FAR = 1 << 20
TILE_HEADS = 4
AXES = ("zh", "y", "c", "zl", "x")
RING_Z = ("zh", "zl")
RING_Y = ("y",)
OFFSETS = (0, -1, 1, 2)

rope_base = 1000000.0
yarn_factor = 4.0
orig_len = 32768.0
beta_fast = 32.0
beta_slow = 1.0
mscale_yarn = 0.1 * math.log(4.0) + 1.0


F32 = jnp.float32
BF16 = jnp.bfloat16
VMEM_LIMIT = 60 * 1024 * 1024


def params(*semantics):
    return pltpu.CompilerParams(
        dimension_semantics=semantics, vmem_limit_bytes=VMEM_LIMIT
    )


def yarn_tables(positions, head_size):
    half_size = head_size // 2
    index_f = jnp.arange(half_size, dtype=jnp.float32)
    pos_freq = rope_base ** (2.0 * index_f / head_size)
    inv_extra = 1.0 / pos_freq
    inv_inter = 1.0 / (yarn_factor * pos_freq)
    low_dim = max(
        math.floor(
            head_size
            * math.log(orig_len / (beta_fast * 2.0 * math.pi))
            / (2.0 * math.log(rope_base))
        ),
        0,
    )
    high_dim = min(
        math.ceil(
            head_size
            * math.log(orig_len / (beta_slow * 2.0 * math.pi))
            / (2.0 * math.log(rope_base))
        ),
        head_size - 1,
    )
    ramp_part = jnp.clip((index_f - low_dim) / max(high_dim - low_dim, 0.001), 0.0, 1.0)
    extra_part = 1.0 - ramp_part
    inverse = inv_inter * (1.0 - extra_part) + inv_extra * extra_part
    angles = positions.astype(jnp.float32)[:, None] * inverse[None, :]
    cos_half = jnp.cos(angles) * mscale_yarn
    sin_half = jnp.sin(angles) * mscale_yarn
    return (
        jnp.concatenate([cos_half, cos_half], axis=-1),
        jnp.concatenate([-sin_half, sin_half], axis=-1),
    )


def rotate_kernel(
    core_ref, q_ref, k_ref, v_ref, cos_ref, sin_ref, keep_ref, give_ref, keep_kv_ref, give_kv_ref
):
    core = core_ref[0]
    cos_t = cos_ref[...]
    sin_t = sin_ref[...]

    def rotated(part):
        value = part.astype(F32)
        return (value * cos_t + pltpu.roll(value, DH // 2, 1) * sin_t).astype(BF16)

    half = keep_ref.shape[1]
    for q_out, kv_out, which in (
        (keep_ref, keep_kv_ref, core),
        (give_ref, give_kv_ref, 1 - core),
    ):
        head_span = pl.ds(pl.multiple_of(which * DH, DH), DH)
        kv_out[:, :DH] = rotated(k_ref[:, head_span])
        kv_out[:, DH:] = v_ref[:, head_span]
        for head in range(half // DH):
            source = pl.ds(pl.multiple_of(which * half + head * DH, DH), DH)
            q_out[:, pl.ds(head * DH, DH)] = rotated(q_ref[:, source])


def rotate_all(core, queries, keys, values, cos_t, sin_t):
    rows, width = queries.shape
    vmem = pl.BlockSpec(memory_space=pltpu.VMEM)
    return pl.pallas_call(
        rotate_kernel,
        in_specs=[pl.BlockSpec(memory_space=pltpu.SMEM)] + [vmem] * 5,
        out_specs=[vmem] * 4,
        out_shape=[jax.ShapeDtypeStruct((rows, width // 2), BF16)] * 2
        + [jax.ShapeDtypeStruct((rows, 2 * DH), BF16)] * 2,
        compiler_params=params(),
        name="rotate_all",
    )(core, queries, keys, values, cos_t, sin_t)


def first_block(z, y, c):
    return z // 2 * 64 + y * 16 + c * 8 + z % 2 * 4


def attend_kernel(meta_ref, theirs_ref, own_ref, *refs, units, pieces, heads, tile_heads, first, last):
    piece_refs, refs = refs[:pieces], refs[pieces:]
    if not first:
        state_in, refs = refs[:3], refs[3:]
    if last:
        out_refs, refs = refs[:2], refs[2:]
    state, refs = refs[:3], refs[3:]
    kv_ref, q_ref, base_ref, list_ref, sem_ref = refs
    unit_rows = UNIT * BLOCK
    copies = []
    place = 0
    for index, piece in enumerate(piece_refs):
        size = piece.shape[0]
        copies.append(
            pltpu.make_async_copy(piece, kv_ref.at[pl.ds(place, size), :], sem_ref.at[index])
        )
        copies[-1].start()
        place += size
    max_ref, sum_ref, acc_ref = state
    if first:
        max_ref[...] = jnp.full_like(max_ref, -1e30)
        sum_ref[...] = jnp.zeros_like(sum_ref)
        acc_ref[...] = jnp.zeros_like(acc_ref)
    else:
        for source, target in zip(state_in, state):
            target[...] = source[...]
    q_ref[0] = theirs_ref[...]
    q_ref[1] = own_ref[...]
    for index, (z_off, y_off, c) in enumerate(units):
        base_ref[index] = first_block((meta_ref[2] + z_off) % 4, (meta_ref[3] + y_off) % 4, c)
    for copy in copies:
        copy.wait()

    factor = math.log2(math.e) / math.sqrt(DH)
    rows = tile_heads * BLOCK
    parts = heads // tile_heads
    keys_len = 2 * unit_rows

    @pl.loop(0, 2)
    def _(which):
        block = meta_ref[which]

        def update(u0, u1, masked):
            starts = [pl.multiple_of(jnp.maximum(u, 0) * unit_rows, unit_rows) for u in (u0, u1)]
            keys = jnp.concatenate([kv_ref[pl.ds(s, unit_rows), :DH] for s in starts], axis=0)
            vals = jnp.concatenate([kv_ref[pl.ds(s, unit_rows), DH:] for s in starts], axis=0)
            if masked:
                bases = [jnp.where(u < 0, FAR, base_ref[jnp.maximum(u, 0)]) for u in (u0, u1)]
                shape = (BLOCK, unit_rows)
                row_token = lax.broadcasted_iota(jnp.int32, shape, 0)
                key_token = lax.broadcasted_iota(jnp.int32, shape, 1)
                allowed = jnp.concatenate(
                    [
                        jnp.where(key_token + (base - block) * BLOCK <= row_token, 1, 0)
                        for base in bases
                    ],
                    axis=1,
                )

            def scores_of(part):
                query = jnp.concatenate(
                    [
                        q_ref[which, :, pl.ds((part * tile_heads + h) * DH, DH)]
                        for h in range(tile_heads)
                    ],
                    axis=0,
                )
                scores = lax.dot_general(
                    query, keys, (((1,), (1,)), ((), ())), preferred_element_type=F32
                )
                if masked:
                    scores = jnp.where(
                        allowed[None] > 0, scores.reshape(tile_heads, BLOCK, keys_len), -1e30
                    ).reshape(rows, keys_len)
                return scores

            def absorb(part, scores):
                start = pl.multiple_of((which * heads + part * tile_heads) * BLOCK, BLOCK)
                span = pl.ds(start, rows)
                old_max = max_ref[span, :]
                new_max = jnp.maximum(old_max, jnp.max(scores, axis=1, keepdims=True))
                decay = jnp.exp2((old_max - new_max) * factor)
                lane_sum = sum_ref[span, :] * decay
                weights = []
                for column in range(keys_len // DH):
                    some = scores[:, column * DH : (column + 1) * DH]
                    piece = jnp.exp2((some - new_max) * factor)
                    lane_sum = lane_sum + piece
                    weights.append(piece.astype(BF16))
                sum_ref[span, :] = lane_sum
                max_ref[span, :] = new_max
                added = jnp.dot(jnp.concatenate(weights, axis=1), vals, preferred_element_type=F32)
                acc_ref[span, :] = acc_ref[span, :] * decay + added

            scores = scores_of(0)
            for part in range(parts):
                later = scores_of(part + 1) if part + 1 < parts else None
                absorb(part, scores)
                scores = later

        count = jnp.int32(0)
        diagonal = jnp.int32(-1)
        for unit in range(len(units)):
            base = base_ref[unit]
            list_ref[count] = unit
            count = count + jnp.where(base + UNIT <= block, 1, 0)
            diagonal = jnp.where(
                jnp.logical_and(base <= block, block < base + UNIT), unit, diagonal
            )
        whole = count // 2

        @pl.loop(0, whole)
        def _(step):
            update(list_ref[2 * step], list_ref[2 * step + 1], False)

        odd = jnp.where(count > 2 * whole, list_ref[jnp.maximum(count - 1, 0)], -1)

        @pl.when(jnp.logical_or(odd >= 0, diagonal >= 0))
        def _():
            update(odd, diagonal, True)

    if last:
        for head in range(2 * heads):
            span = pl.ds(head * BLOCK, BLOCK)
            total = jnp.sum(sum_ref[span, :], axis=1, keepdims=True)
            out_refs[head // heads][:, pl.ds(head % heads * DH, DH)] = (
                acc_ref[span, :] / total
            ).astype(BF16)


def attend(meta, units, theirs, own, pieces, state=None, last=False, tile_heads=TILE_HEADS):
    rows, width = own.shape
    heads = width // DH
    vmem = pl.BlockSpec(memory_space=pltpu.VMEM)
    states = [(2 * heads * rows, DH)] * 3
    scratch = [
        pltpu.VMEM((len(units) * UNIT * BLOCK, 2 * DH), BF16),
        pltpu.VMEM((2, rows, width), BF16),
        pltpu.SMEM((len(units),), jnp.int32),
        pltpu.SMEM((len(units) + 1,), jnp.int32),
        pltpu.SemaphoreType.DMA((len(pieces),)),
    ]
    if last:
        scratch = [pltpu.VMEM(shape, F32) for shape in states] + scratch
        out_shape = [jax.ShapeDtypeStruct((rows, width), BF16)] * 2
    else:
        out_shape = [jax.ShapeDtypeStruct(shape, F32) for shape in states]
    state = [] if state is None else list(state)
    kernel = functools.partial(
        attend_kernel,
        units=units,
        pieces=len(pieces),
        heads=heads,
        tile_heads=tile_heads,
        first=not state,
        last=last,
    )
    keys_seen = len(units) * UNIT * BLOCK
    return pl.pallas_call(
        kernel,
        in_specs=[pl.BlockSpec(memory_space=pltpu.SMEM), vmem, vmem]
        + [pl.BlockSpec(memory_space=pl.ANY)] * len(pieces)
        + [vmem] * len(state),
        out_specs=[vmem] * len(out_shape),
        out_shape=out_shape,
        scratch_shapes=scratch,
        compiler_params=params(),
        cost_estimate=pl.CostEstimate(
            flops=4 * keys_seen * heads * rows * DH,
            bytes_accessed=keys_seen * 4 * DH,
            transcendentals=keys_seen * heads * rows,
        ),
        name="attend_last" if last else "attend_more" if state else "attend_first",
    )(meta, theirs, own, *pieces, *state)


def slots_of(ids_ref):
    shape = (BLOCK, BLOCK)
    expert = lax.broadcasted_iota(jnp.int32, shape, 0)
    named = jnp.zeros(shape, F32)
    for k in range(TOP):
        named = named + jnp.where(ids_ref[k : k + 1, :] == expert, 1.0, 0.0)
    earlier = jnp.where(
        lax.broadcasted_iota(jnp.int32, shape, 0) < lax.broadcasted_iota(jnp.int32, shape, 1),
        1.0,
        0.0,
    )
    counts = jnp.dot(named.astype(BF16), earlier.astype(BF16), preferred_element_type=F32)
    return named, jnp.where(named > 0.0, counts, -1.0)


def own_kernel(core_ref, own_ref, w_ref, out_ref):
    @pl.when(pl.program_id(0) == 0)
    def _():
        out_ref[...] = jnp.zeros_like(out_ref)

    depth = w_ref.shape[0]
    column = pl.ds(pl.multiple_of(pl.program_id(0) * depth, depth), depth)
    out_ref[...] += jnp.dot(own_ref[:, column], w_ref[...], preferred_element_type=F32)


def project_own(core, own, w_out, depth=512):
    rows, half = own.shape
    width = w_out.shape[1]
    steps = half // depth
    return pl.pallas_call(
        own_kernel,
        grid_spec=pltpu.PrefetchScalarGridSpec(
            num_scalar_prefetch=1,
            grid=(steps,),
            in_specs=[
                pl.BlockSpec((rows, half), lambda step, core_ref: (0, 0)),
                pl.BlockSpec((depth, width), lambda step, core_ref: (core_ref[0] * steps + step, 0)),
            ],
            out_specs=pl.BlockSpec((rows, width), lambda step, core_ref: (0, 0)),
        ),
        out_shape=jax.ShapeDtypeStruct((rows, width), F32),
        compiler_params=params("arbitrary"),
        cost_estimate=pl.CostEstimate(
            flops=2 * rows * half * width, bytes_accessed=2 * half * width, transcendentals=0
        ),
        name="project_own",
    )(core, own, w_out)


def project_kernel(
    core_ref, part_ref, got_ref, w_ref, hidden_ref, gain_ref, router_ref, ids_ref,
    h1_ref, slot_ref, route_ref, send_ref, acc_ref, hn_ref, pick_ref, over_ref, *, steps,
):
    step = pl.program_id(0)
    depth = w_ref.shape[0]
    tiles = hn_ref.shape[1] // DH

    @pl.when(step == 0)
    def _():
        acc_ref[...] = part_ref[...] + hidden_ref[...].astype(F32)

    @pl.when(step < steps)
    def _():
        column = pl.ds(pl.multiple_of(step * depth, depth), depth)
        acc_ref[...] += jnp.dot(got_ref[:, column], w_ref[...], preferred_element_type=F32)

    @pl.when(step == steps - 1)
    def _():
        h1 = acc_ref[...].astype(BF16)
        h1_ref[...] = h1
        h1_f = h1.astype(F32)
        mean = jnp.mean(h1_f * h1_f, axis=-1, keepdims=True)
        hn = (h1_f / jnp.sqrt(mean + 1e-06) * gain_ref[...]).astype(BF16)
        hn_ref[...] = hn
        logits = jnp.dot(hn, router_ref[...], preferred_element_type=F32)
        named, slot = slots_of(ids_ref)
        slot_ref[...] = slot
        raised = jnp.where(named > 0.0, jnp.exp(jnp.transpose(logits)), 0.0)
        route_ref[...] = raised / jnp.sum(raised, axis=0, keepdims=True)
        wanted = lax.broadcasted_iota(jnp.int32, (BLOCK, MAIN, BLOCK), 1).astype(F32)
        pick = jnp.where(slot[:, None, :] == wanted, 1.0, 0.0).reshape(BLOCK * MAIN, BLOCK)
        pick_ref[...] = pick.astype(BF16)
        last = jnp.where(slot == float(MAIN), 1.0, 0.0).astype(BF16)
        for tile in range(tiles):
            part = hn[:, tile * DH : (tile + 1) * DH]
            over_ref[:, tile, :] = jnp.dot(last, part, preferred_element_type=F32)

    stripe = send_ref.shape[1] // MAIN
    for index in range(pl.cdiv(tiles, stripe)):

        @pl.when(step == steps + index)
        def _(index=index):
            first = index * stripe
            held = min(stripe, tiles - first)
            columns = hn_ref[:, first * DH : (first + held) * DH]
            rows = jnp.dot(pick_ref[...], columns, preferred_element_type=F32)
            send_ref[:, : held * MAIN, :] = tiled_rows(rows)
            if held < stripe:
                send_ref[:, held * MAIN :, :] = over_ref[...].astype(BF16)


def tiled_rows(rows):
    sources = rows.shape[0] // MAIN
    pieces = [
        rows[:, tile * DH : (tile + 1) * DH].reshape(sources, MAIN, DH)
        for tile in range(rows.shape[1] // DH)
    ]
    return jnp.concatenate(pieces, axis=1).astype(BF16)


def project(core, part, got, w_out, hidden, gain, w_router, ids_t, depth=512):
    rows, half = got.shape
    width = hidden.shape[1]
    steps = half // depth
    experts = w_router.shape[1]
    tiles = width // DH
    packed = (experts, tiles * CAP, DH)
    over = (experts, tiles, DH)

    def full(shape):
        return pl.BlockSpec(shape, lambda step, core_ref: (0,) * len(shape))

    def w_map(step, core_ref):
        return (1 - core_ref[0]) * steps + jnp.minimum(step, steps - 1), 0

    return pl.pallas_call(
        functools.partial(project_kernel, steps=steps),
        grid_spec=pltpu.PrefetchScalarGridSpec(
            num_scalar_prefetch=1,
            grid=(steps + packed[1] // STRIPE,),
            in_specs=[
                full((rows, width)),
                full((rows, half)),
                pl.BlockSpec((depth, width), w_map),
                full((rows, width)),
                full((1, width)),
                full((width, experts)),
                full((TOP, rows)),
            ],
            out_specs=[
                full((rows, width)),
                full((experts, rows)),
                full((experts, rows)),
                pl.BlockSpec(
                    (experts, STRIPE, DH),
                    lambda step, core_ref: (0, jnp.maximum(step - steps, 0), 0),
                ),
            ],
            scratch_shapes=[
                pltpu.VMEM((rows, width), F32),
                pltpu.VMEM((rows, width), BF16),
                pltpu.VMEM((experts * MAIN, rows), BF16),
                pltpu.VMEM(over, F32),
            ],
        ),
        out_shape=[
            jax.ShapeDtypeStruct((rows, width), BF16),
            jax.ShapeDtypeStruct((experts, rows), F32),
            jax.ShapeDtypeStruct((experts, rows), F32),
            jax.ShapeDtypeStruct(packed, BF16),
        ],
        compiler_params=params("arbitrary"),
        name="project",
    )(core, part, got, w_out, hidden, gain, w_router, ids_t)


def expert_kernel(
    in_ref, gate_ref, up_ref, down_ref, out_ref, rows_ref, act_ref, over_ref, *, steps, up_steps
):
    step = pl.program_id(0)
    tile = gate_ref.shape[1]
    sources = in_ref.shape[0]
    main_rows = sources * MAIN
    tiles = gate_ref.shape[0] // DH
    stripe = in_ref.shape[1] // MAIN
    third = sources * CAP // 3

    for index in range(steps):

        @pl.when(step == index)
        def _(index=index):
            first = index * stripe
            held = min(stripe, tiles - first)
            for place in range(held):
                columns = pl.ds((first + place) * DH, DH)
                rows_ref[:main_rows, columns] = in_ref[
                    :, place * MAIN : (place + 1) * MAIN, :
                ].reshape(main_rows, DH)
            if held < stripe:
                over_ref[...] = in_ref[:, held * MAIN :, :].astype(F32)
                for place in range(tiles):
                    columns = pl.ds(place * DH, DH)
                    rows_ref[main_rows:, columns] = over_ref[:, place, :].astype(BF16)

    for index in range(up_steps):

        @pl.when(step == steps + index)
        def _(index=index):
            for start in range(0, 3 * third, third):
                rows = rows_ref[start : start + third, :]
                gate = jnp.dot(rows, gate_ref[...], preferred_element_type=F32)
                up = jnp.dot(rows, up_ref[...], preferred_element_type=F32)
                act = gate / (1.0 + jnp.exp(-gate)) * up
                act_ref[start : start + third, index * tile : (index + 1) * tile] = act.astype(BF16)

    for index in range(steps):

        @pl.when(step == steps + up_steps + index)
        def _(index=index):
            first = index * stripe
            held = min(stripe, tiles - first)
            for start in range(0, 3 * third, third):
                rows = jnp.dot(
                    act_ref[start : start + third, :],
                    down_ref[:, : held * DH],
                    preferred_element_type=F32,
                )
                some = min(third, main_rows - start)
                out_ref[start // MAIN : (start + some) // MAIN, : held * MAIN, :] = tiled_rows(
                    rows[:some]
                )
                if some < third:
                    for place in range(held):
                        over_ref[:, first + place, :] = rows[some:, place * DH : (place + 1) * DH]
            if held < stripe:
                out_ref[:, held * MAIN :, :] = over_ref[...].astype(BF16)


def experts_of(packed, w_gate, w_up, w_down):
    sources = packed.shape[0]
    width, hidden_units = w_gate.shape
    tile = 256
    steps = packed.shape[1] // STRIPE
    up_steps = hidden_units // tile
    rows = sources * CAP

    def out_step(step):
        return jnp.maximum(step - steps - up_steps, 0)

    def up_map(step):
        return 0, jnp.clip(step - steps, 0, up_steps - 1)

    return pl.pallas_call(
        functools.partial(expert_kernel, steps=steps, up_steps=up_steps),
        grid=(2 * steps + up_steps,),
        in_specs=[
            pl.BlockSpec((sources, STRIPE, DH), lambda step: (0, jnp.minimum(step, steps - 1), 0)),
            pl.BlockSpec((width, tile), up_map),
            pl.BlockSpec((width, tile), up_map),
            pl.BlockSpec((hidden_units, STRIPE // MAIN * DH), lambda step: (0, out_step(step))),
        ],
        out_specs=pl.BlockSpec((sources, STRIPE, DH), lambda step: (0, out_step(step), 0)),
        out_shape=jax.ShapeDtypeStruct(packed.shape, BF16),
        scratch_shapes=[
            pltpu.VMEM((rows, width), BF16),
            pltpu.VMEM((rows, hidden_units), BF16),
            pltpu.VMEM((sources, width // DH, DH), F32),
        ],
        compiler_params=params("arbitrary"),
        name="experts_of",
    )(packed, w_gate, w_up, w_down)


def combine_kernel(
    slot_ref, route_ref, in_ref, in_over_ref, h1_ref, out_ref, mix_ref, last_ref, over_ref, *, tiles
):
    step = pl.program_id(0)
    stripe = in_ref.shape[1] // MAIN

    @pl.when(step == 0)
    def _():
        slot = slot_ref[...]
        route = route_ref[...]
        wanted = lax.broadcasted_iota(jnp.int32, (BLOCK, MAIN, BLOCK), 1).astype(F32)
        mix = jnp.where(slot[:, None, :] == wanted, route[:, None, :], 0.0)
        mix_ref[...] = jnp.transpose(mix.reshape(BLOCK * MAIN, BLOCK).astype(BF16))
        last_ref[...] = jnp.transpose(jnp.where(slot == float(MAIN), route, 0.0)).astype(BF16)
        over_ref[...] = in_over_ref[...].astype(F32)

    for index in range(pl.cdiv(tiles, stripe)):

        @pl.when(step == index)
        def _(index=index):
            first = index * stripe
            held = min(stripe, tiles - first)
            rows = jnp.concatenate(
                [
                    in_ref[:, p * MAIN : (p + 1) * MAIN, :].reshape(BLOCK * MAIN, DH)
                    for p in range(held)
                ],
                axis=1,
            )
            extra = jnp.concatenate(
                [over_ref[:, first + p, :].astype(BF16) for p in range(held)], axis=1
            )
            total = jnp.dot(mix_ref[...], rows, preferred_element_type=F32)
            total = total + jnp.dot(last_ref[...], extra, preferred_element_type=F32)
            columns = slice(first * DH, (first + held) * DH)
            out_ref[:, columns] = (total + h1_ref[:, columns].astype(F32)).astype(BF16)


def combine(slot, route, packed, h1):
    rows, width = h1.shape
    experts = packed.shape[0]
    tiles = width // DH

    def whole(shape):
        return pl.BlockSpec(shape, lambda step: (0,) * len(shape))

    return pl.pallas_call(
        functools.partial(combine_kernel, tiles=tiles),
        grid=(packed.shape[1] // STRIPE,),
        in_specs=[
            whole(slot.shape),
            whole(route.shape),
            pl.BlockSpec((experts, STRIPE, DH), lambda step: (0, step, 0)),
            pl.BlockSpec((experts, tiles, DH), lambda step: (0, MAIN, 0)),
            whole(h1.shape),
        ],
        out_specs=whole(h1.shape),
        out_shape=jax.ShapeDtypeStruct((rows, width), BF16),
        scratch_shapes=[
            pltpu.VMEM((rows, experts * MAIN), BF16),
            pltpu.VMEM((rows, experts), BF16),
            pltpu.VMEM((experts, tiles, DH), F32),
        ],
        compiler_params=params("arbitrary"),
        name="combine",
    )(slot, route, packed, packed, h1)


def exchange(packed):
    return lax.all_to_all(packed, AXES, split_axis=0, concat_axis=0, tiled=True)


def ring_near(piece, axes):
    left = lax.ppermute(piece, axes, [(i, (i + 1) % 4) for i in range(4)])
    right = lax.ppermute(piece, axes, [(i, (i + 3) % 4) for i in range(4)])
    return left, right


def ring_far(left, right, axes):
    half = left.shape[0] // 2
    low = lax.ppermute(left[:half], axes, [(i, (i + 1) % 4) for i in range(4)])
    high = lax.ppermute(right[half:], axes, [(i, (i + 3) % 4) for i in range(4)])
    return low, high


def ring_gather(piece, axes):
    left, right = ring_near(piece, axes)
    far = lax.ppermute(piece, axes, [(i, (i + 2) % 4) for i in range(4)])
    return jnp.concatenate([piece, left, right, far], axis=0)


def local(
    hidden, queries, keys, values, w_out, norm_gain, w_router, expert_ids, w_gate, w_up, w_down
):
    rows = hidden.shape[0]
    device = lax.axis_index(AXES)
    core = lax.axis_index("c")
    positions = device * rows + jnp.arange(rows, dtype=jnp.int32)
    cos_t, sin_t = yarn_tables(positions, DH)
    core_arr = core.reshape(1).astype(jnp.int32)
    keep, give, keep_kv, give_kv = rotate_all(core_arr, queries, keys, values, cos_t, sin_t)
    mirror = [(i, BLOCKS - 1 - i) for i in range(BLOCKS)]
    taken = lax.ppermute(give, AXES, mirror)
    other_kv = lax.ppermute(give_kv, ("c",), [(0, 1), (1, 0)])
    is_low = core == 0
    chip = jnp.concatenate(
        [jnp.where(is_low, keep_kv, other_kv), jnp.where(is_low, other_kv, keep_kv)], axis=0
    )
    row = lax.all_gather(chip, ("x",), axis=0)
    low = row[:, :rows].reshape(UNIT * rows, 2 * DH)
    high = row[:, rows:].reshape(UNIT * rows, 2 * DH)
    low = ring_gather(low, RING_Y)
    high = ring_gather(high, RING_Z)
    low_near = ring_near(low, RING_Z)
    high_near = ring_near(high, RING_Y)
    low_far = ring_far(*low_near, RING_Z)
    high_far = ring_far(*high_near, RING_Y)

    def units(order):
        return [(outer, inner, 0) for outer in order for inner in OFFSETS] + [
            (inner, outer, 1) for outer in order for inner in OFFSETS
        ]

    meta = jnp.stack(
        [BLOCKS - 1 - device, device, lax.axis_index(RING_Z), lax.axis_index(RING_Y)]
    ).astype(jnp.int32)
    state = attend(meta, units((0,)), taken, keep, [low, high])
    state = attend(meta, units((-1, 1)), taken, keep, [*low_near, *high_near], state=state)
    theirs, own = attend(
        meta, units((2,)), taken, keep, [*low_far, *high_far], state=state, last=True
    )
    got = lax.ppermute(theirs, AXES, mirror)
    part = project_own(core_arr, own, w_out)
    h1, slot, route, packed = project(
        core_arr, part, got, w_out, hidden, norm_gain[None, :], w_router, expert_ids.T
    )
    returned = exchange(experts_of(exchange(packed), w_gate[0], w_up[0], w_down[0]))
    return combine(slot, route, returned, h1)


def solution(mesh):
    torus = Mesh(mesh.devices.reshape(2, 4, 2, 2, 4), AXES)
    split = P(AXES, None)
    experts = P(AXES, None, None)
    in_specs = (
        split, split, split, split, P(), P(), P(), split, experts, experts, experts,
    )
    return jax.shard_map(local, mesh=torus, in_specs=in_specs, out_specs=split, check_vma=False)
```

```python
import functools
import math

import jax
import jax.numpy as jnp
from jax import lax
from jax.experimental import pallas as pl
from jax.experimental.pallas import tpu as pltpu
from jax.sharding import Mesh, PartitionSpec as P


DH = 128
TOP = 8
CAP = 9
MAIN = 8
STRIPE = 48
BLOCK = 128
BLOCKS = 128
UNIT = 4
FAR = 1 << 20
TILE_HEADS = 4
AXES = ("zh", "y", "c", "zl", "x")
TORUS = ("zh", "zl", "y", "x", "c")
RING_Z = ("zh", "zl")
RING_Y = ("y",)
OFFSETS = (0, -1, 1, 2)

rope_base = 1000000.0
yarn_factor = 4.0
orig_len = 32768.0
beta_fast = 32.0
beta_slow = 1.0
mscale_yarn = 0.1 * math.log(4.0) + 1.0


F32 = jnp.float32
BF16 = jnp.bfloat16
VMEM_LIMIT = 60 * 1024 * 1024


def params(*semantics):
    return pltpu.CompilerParams(
        dimension_semantics=semantics, vmem_limit_bytes=VMEM_LIMIT
    )


def yarn_tables(positions, head_size):
    half_size = head_size // 2
    index_f = jnp.arange(half_size, dtype=jnp.float32)
    pos_freq = rope_base ** (2.0 * index_f / head_size)
    inv_extra = 1.0 / pos_freq
    inv_inter = 1.0 / (yarn_factor * pos_freq)
    low_dim = max(
        math.floor(
            head_size
            * math.log(orig_len / (beta_fast * 2.0 * math.pi))
            / (2.0 * math.log(rope_base))
        ),
        0,
    )
    high_dim = min(
        math.ceil(
            head_size
            * math.log(orig_len / (beta_slow * 2.0 * math.pi))
            / (2.0 * math.log(rope_base))
        ),
        head_size - 1,
    )
    ramp_part = jnp.clip((index_f - low_dim) / max(high_dim - low_dim, 0.001), 0.0, 1.0)
    extra_part = 1.0 - ramp_part
    inverse = inv_inter * (1.0 - extra_part) + inv_extra * extra_part
    angles = positions.astype(jnp.float32)[:, None] * inverse[None, :]
    cos_half = jnp.cos(angles) * mscale_yarn
    sin_half = jnp.sin(angles) * mscale_yarn
    return (
        jnp.concatenate([cos_half, cos_half], axis=-1),
        jnp.concatenate([-sin_half, sin_half], axis=-1),
    )


def rotate_kernel(
    core_ref, q_ref, k_ref, v_ref, cos_ref, sin_ref, keep_ref, give_ref, keep_kv_ref, give_kv_ref
):
    core = core_ref[0]
    cos_t = cos_ref[...]
    sin_t = sin_ref[...]

    def rotated(part):
        value = part.astype(F32)
        return (value * cos_t + pltpu.roll(value, DH // 2, 1) * sin_t).astype(BF16)

    half = keep_ref.shape[1]
    for q_out, kv_out, which in (
        (keep_ref, keep_kv_ref, core),
        (give_ref, give_kv_ref, 1 - core),
    ):
        head_span = pl.ds(pl.multiple_of(which * DH, DH), DH)
        kv_out[:, :DH] = rotated(k_ref[:, head_span])
        kv_out[:, DH:] = v_ref[:, head_span]
        for head in range(half // DH):
            source = pl.ds(pl.multiple_of(which * half + head * DH, DH), DH)
            q_out[:, pl.ds(head * DH, DH)] = rotated(q_ref[:, source])


def rotate_all(core, queries, keys, values, cos_t, sin_t):
    rows, width = queries.shape
    vmem = pl.BlockSpec(memory_space=pltpu.VMEM)
    return pl.pallas_call(
        rotate_kernel,
        in_specs=[pl.BlockSpec(memory_space=pltpu.SMEM)] + [vmem] * 5,
        out_specs=[vmem] * 4,
        out_shape=[jax.ShapeDtypeStruct((rows, width // 2), BF16)] * 2
        + [jax.ShapeDtypeStruct((rows, 2 * DH), BF16)] * 2,
        compiler_params=params(),
        name="rotate_all",
    )(core, queries, keys, values, cos_t, sin_t)


def first_block(z, y, c):
    return z // 2 * 64 + y * 16 + c * 8 + z % 2 * 4


def attend_kernel(meta_ref, theirs_ref, own_ref, *refs, units, pieces, heads, tile_heads, first, last):
    piece_refs, refs = refs[:pieces], refs[pieces:]
    if not first:
        state_in, refs = refs[:3], refs[3:]
    if last:
        out_refs, refs = refs[:2], refs[2:]
    state, refs = refs[:3], refs[3:]
    kv_ref, q_ref, base_ref, list_ref, sem_ref = refs
    unit_rows = UNIT * BLOCK
    copies = []
    place = 0
    for index, piece in enumerate(piece_refs):
        size = piece.shape[0]
        copies.append(
            pltpu.make_async_copy(piece, kv_ref.at[pl.ds(place, size), :], sem_ref.at[index])
        )
        copies[-1].start()
        place += size
    max_ref, sum_ref, acc_ref = state
    if first:
        max_ref[...] = jnp.full_like(max_ref, -1e30)
        sum_ref[...] = jnp.zeros_like(sum_ref)
        acc_ref[...] = jnp.zeros_like(acc_ref)
    else:
        for source, target in zip(state_in, state):
            target[...] = source[...]
    q_ref[0] = theirs_ref[...]
    q_ref[1] = own_ref[...]
    for index, (z_off, y_off, c) in enumerate(units):
        base_ref[index] = first_block((meta_ref[2] + z_off) % 4, (meta_ref[3] + y_off) % 4, c)
    for copy in copies:
        copy.wait()

    factor = math.log2(math.e) / math.sqrt(DH)
    rows = tile_heads * BLOCK
    parts = heads // tile_heads
    keys_len = 2 * unit_rows

    @pl.loop(0, 2)
    def _(which):
        block = meta_ref[which]

        def update(u0, u1, masked):
            starts = [pl.multiple_of(jnp.maximum(u, 0) * unit_rows, unit_rows) for u in (u0, u1)]
            keys = jnp.concatenate([kv_ref[pl.ds(s, unit_rows), :DH] for s in starts], axis=0)
            vals = jnp.concatenate([kv_ref[pl.ds(s, unit_rows), DH:] for s in starts], axis=0)
            if masked:
                bases = [jnp.where(u < 0, FAR, base_ref[jnp.maximum(u, 0)]) for u in (u0, u1)]
                shape = (BLOCK, unit_rows)
                row_token = lax.broadcasted_iota(jnp.int32, shape, 0)
                key_token = lax.broadcasted_iota(jnp.int32, shape, 1)
                allowed = jnp.concatenate(
                    [
                        jnp.where(key_token + (base - block) * BLOCK <= row_token, 1, 0)
                        for base in bases
                    ],
                    axis=1,
                )

            def scores_of(part):
                query = jnp.concatenate(
                    [
                        q_ref[which, :, pl.ds((part * tile_heads + h) * DH, DH)]
                        for h in range(tile_heads)
                    ],
                    axis=0,
                )
                scores = lax.dot_general(
                    query, keys, (((1,), (1,)), ((), ())), preferred_element_type=F32
                )
                if masked:
                    scores = jnp.where(
                        allowed[None] > 0, scores.reshape(tile_heads, BLOCK, keys_len), -1e30
                    ).reshape(rows, keys_len)
                return scores

            def absorb(part, scores):
                start = pl.multiple_of((which * heads + part * tile_heads) * BLOCK, BLOCK)
                span = pl.ds(start, rows)
                old_max = max_ref[span, :]
                new_max = jnp.maximum(old_max, jnp.max(scores, axis=1, keepdims=True))
                decay = jnp.exp2((old_max - new_max) * factor)
                lane_sum = sum_ref[span, :] * decay
                weights = []
                for column in range(keys_len // DH):
                    some = scores[:, column * DH : (column + 1) * DH]
                    piece = jnp.exp2((some - new_max) * factor)
                    lane_sum = lane_sum + piece
                    weights.append(piece.astype(BF16))
                sum_ref[span, :] = lane_sum
                max_ref[span, :] = new_max
                added = jnp.dot(jnp.concatenate(weights, axis=1), vals, preferred_element_type=F32)
                acc_ref[span, :] = acc_ref[span, :] * decay + added

            scores = scores_of(0)
            for part in range(parts):
                later = scores_of(part + 1) if part + 1 < parts else None
                absorb(part, scores)
                scores = later

        count = jnp.int32(0)
        diagonal = jnp.int32(-1)
        for unit in range(len(units)):
            base = base_ref[unit]
            list_ref[count] = unit
            count = count + jnp.where(base + UNIT <= block, 1, 0)
            diagonal = jnp.where(
                jnp.logical_and(base <= block, block < base + UNIT), unit, diagonal
            )
        whole = count // 2

        @pl.loop(0, whole)
        def _(step):
            update(list_ref[2 * step], list_ref[2 * step + 1], False)

        odd = jnp.where(count > 2 * whole, list_ref[jnp.maximum(count - 1, 0)], -1)

        @pl.when(jnp.logical_or(odd >= 0, diagonal >= 0))
        def _():
            update(odd, diagonal, True)

    if last:
        for head in range(2 * heads):
            span = pl.ds(head * BLOCK, BLOCK)
            total = jnp.sum(sum_ref[span, :], axis=1, keepdims=True)
            out_refs[head // heads][:, pl.ds(head % heads * DH, DH)] = (
                acc_ref[span, :] / total
            ).astype(BF16)


def attend(meta, units, theirs, own, pieces, state=None, last=False, tile_heads=TILE_HEADS):
    rows, width = own.shape
    heads = width // DH
    vmem = pl.BlockSpec(memory_space=pltpu.VMEM)
    states = [(2 * heads * rows, DH)] * 3
    scratch = [
        pltpu.VMEM((len(units) * UNIT * BLOCK, 2 * DH), BF16),
        pltpu.VMEM((2, rows, width), BF16),
        pltpu.SMEM((len(units),), jnp.int32),
        pltpu.SMEM((len(units) + 1,), jnp.int32),
        pltpu.SemaphoreType.DMA((len(pieces),)),
    ]
    if last:
        scratch = [pltpu.VMEM(shape, F32) for shape in states] + scratch
        out_shape = [jax.ShapeDtypeStruct((rows, width), BF16)] * 2
    else:
        out_shape = [jax.ShapeDtypeStruct(shape, F32) for shape in states]
    state = [] if state is None else list(state)
    kernel = functools.partial(
        attend_kernel,
        units=units,
        pieces=len(pieces),
        heads=heads,
        tile_heads=tile_heads,
        first=not state,
        last=last,
    )
    keys_seen = len(units) * UNIT * BLOCK
    return pl.pallas_call(
        kernel,
        in_specs=[pl.BlockSpec(memory_space=pltpu.SMEM), vmem, vmem]
        + [pl.BlockSpec(memory_space=pl.ANY)] * len(pieces)
        + [vmem] * len(state),
        out_specs=[vmem] * len(out_shape),
        out_shape=out_shape,
        scratch_shapes=scratch,
        compiler_params=params(),
        cost_estimate=pl.CostEstimate(
            flops=4 * keys_seen * heads * rows * DH,
            bytes_accessed=keys_seen * 4 * DH,
            transcendentals=keys_seen * heads * rows,
        ),
        name="attend_last" if last else "attend_more" if state else "attend_first",
    )(meta, theirs, own, *pieces, *state)


def slots_of(ids_ref):
    shape = (BLOCK, BLOCK)
    expert = lax.broadcasted_iota(jnp.int32, shape, 0)
    named = jnp.zeros(shape, F32)
    for k in range(TOP):
        named = named + jnp.where(ids_ref[k : k + 1, :] == expert, 1.0, 0.0)
    earlier = jnp.where(
        lax.broadcasted_iota(jnp.int32, shape, 0) < lax.broadcasted_iota(jnp.int32, shape, 1),
        1.0,
        0.0,
    )
    counts = jnp.dot(named.astype(BF16), earlier.astype(BF16), preferred_element_type=F32)
    return named, jnp.where(named > 0.0, counts, -1.0)


def own_kernel(core_ref, own_ref, w_ref, out_ref):
    @pl.when(pl.program_id(0) == 0)
    def _():
        out_ref[...] = jnp.zeros_like(out_ref)

    depth = w_ref.shape[0]
    column = pl.ds(pl.multiple_of(pl.program_id(0) * depth, depth), depth)
    out_ref[...] += jnp.dot(own_ref[:, column], w_ref[...], preferred_element_type=F32)


def project_own(core, own, w_out, depth=512):
    rows, half = own.shape
    width = w_out.shape[1]
    steps = half // depth
    return pl.pallas_call(
        own_kernel,
        grid_spec=pltpu.PrefetchScalarGridSpec(
            num_scalar_prefetch=1,
            grid=(steps,),
            in_specs=[
                pl.BlockSpec((rows, half), lambda step, core_ref: (0, 0)),
                pl.BlockSpec((depth, width), lambda step, core_ref: (core_ref[0] * steps + step, 0)),
            ],
            out_specs=pl.BlockSpec((rows, width), lambda step, core_ref: (0, 0)),
        ),
        out_shape=jax.ShapeDtypeStruct((rows, width), F32),
        compiler_params=params("arbitrary"),
        cost_estimate=pl.CostEstimate(
            flops=2 * rows * half * width, bytes_accessed=2 * half * width, transcendentals=0
        ),
        name="project_own",
    )(core, own, w_out)


def torus_place(expert):
    zh, y, c = expert // 64, expert // 16 % 4, expert // 8 % 2
    zl, x = expert // 4 % 2, expert % 4
    return zh * 64 + zl * 32 + y * 8 + x * 2 + c


def plan_kernel(ids_ref, slot_ref, pick_ref, last_ref):
    slot = slots_of(ids_ref)[1]
    slot_ref[...] = slot
    wanted = lax.broadcasted_iota(jnp.int32, (BLOCK, MAIN, BLOCK), 1).astype(F32)
    pick = jnp.where(slot[:, None, :] == wanted, 1.0, 0.0).reshape(BLOCK * MAIN, BLOCK)
    pick_ref[...] = pick.astype(BF16)
    last_ref[...] = jnp.where(slot == float(MAIN), 1.0, 0.0).astype(BF16)


def plan(places_t):
    rows = places_t.shape[1]
    vmem = pl.BlockSpec(memory_space=pltpu.VMEM)
    return pl.pallas_call(
        plan_kernel,
        in_specs=[vmem],
        out_specs=[vmem] * 3,
        out_shape=[
            jax.ShapeDtypeStruct((BLOCKS, rows), F32),
            jax.ShapeDtypeStruct((BLOCKS * MAIN, rows), BF16),
            jax.ShapeDtypeStruct((BLOCKS, rows), BF16),
        ],
        compiler_params=params(),
        name="plan",
    )(places_t)


def routes_kernel(hn_ref, router_ref, ids_ref, slot_ref, mix_ref, last_ref):
    logits = jnp.dot(hn_ref[...], router_ref[...], preferred_element_type=F32)
    named = slots_of(ids_ref)[0]
    raised = jnp.where(named > 0.0, jnp.exp(jnp.transpose(logits)), 0.0)
    by_expert = (raised / jnp.sum(raised, axis=0, keepdims=True)).astype(BF16)
    shape = (BLOCK, BLOCK)
    place = torus_place(lax.broadcasted_iota(jnp.int32, shape, 1))
    order = jnp.where(place == lax.broadcasted_iota(jnp.int32, shape, 0), 1.0, 0.0)
    route = jnp.dot(order.astype(BF16), by_expert, preferred_element_type=F32)
    slot = slot_ref[...]
    wanted = lax.broadcasted_iota(jnp.int32, (BLOCK, MAIN, BLOCK), 1).astype(F32)
    mix = jnp.where(slot[:, None, :] == wanted, route[:, None, :], 0.0)
    mix_ref[...] = jnp.transpose(mix.reshape(BLOCK * MAIN, BLOCK).astype(BF16))
    last_ref[...] = jnp.transpose(jnp.where(slot == float(MAIN), route, 0.0)).astype(BF16)


def routes(hn, w_router, ids_t, slot):
    rows = hn.shape[0]
    vmem = pl.BlockSpec(memory_space=pltpu.VMEM)
    return pl.pallas_call(
        routes_kernel,
        in_specs=[vmem] * 4,
        out_specs=[vmem] * 2,
        out_shape=[
            jax.ShapeDtypeStruct((rows, BLOCKS * MAIN), BF16),
            jax.ShapeDtypeStruct((rows, BLOCKS), BF16),
        ],
        compiler_params=params(),
        name="routes",
    )(hn, w_router, ids_t, slot)


def project_kernel(
    core_ref, part_ref, got_ref, w_ref, hidden_ref, gain_ref, pick_ref, last_ref,
    h1_ref, hn_ref, send_ref, acc_ref, over_ref, *, steps,
):
    step = pl.program_id(0)
    depth = w_ref.shape[0]
    tiles = hn_ref.shape[1] // DH

    @pl.when(step == 0)
    def _():
        acc_ref[...] = part_ref[...] + hidden_ref[...].astype(F32)

    @pl.when(step < steps)
    def _():
        column = pl.ds(pl.multiple_of(step * depth, depth), depth)
        acc_ref[...] += jnp.dot(got_ref[:, column], w_ref[...], preferred_element_type=F32)

    @pl.when(step == steps - 1)
    def _():
        h1 = acc_ref[...].astype(BF16)
        h1_ref[...] = h1
        h1_f = h1.astype(F32)
        mean = jnp.mean(h1_f * h1_f, axis=-1, keepdims=True)
        hn = (h1_f / jnp.sqrt(mean + 1e-06) * gain_ref[...]).astype(BF16)
        hn_ref[...] = hn
        for tile in range(tiles):
            part = hn[:, tile * DH : (tile + 1) * DH]
            over_ref[:, tile, :] = jnp.dot(last_ref[...], part, preferred_element_type=F32)

    stripe = send_ref.shape[1] // MAIN
    for index in range(pl.cdiv(tiles, stripe)):

        @pl.when(step == steps + index)
        def _(index=index):
            first = index * stripe
            held = min(stripe, tiles - first)
            columns = hn_ref[:, first * DH : (first + held) * DH]
            rows = jnp.dot(pick_ref[...], columns, preferred_element_type=F32)
            send_ref[:, : held * MAIN, :] = tiled_rows(rows)
            if held < stripe:
                send_ref[:, held * MAIN :, :] = over_ref[...].astype(BF16)


def tiled_rows(rows):
    sources = rows.shape[0] // MAIN
    pieces = [
        rows[:, tile * DH : (tile + 1) * DH].reshape(sources, MAIN, DH)
        for tile in range(rows.shape[1] // DH)
    ]
    return jnp.concatenate(pieces, axis=1).astype(BF16)


def project(core, part, got, w_out, hidden, gain, pick, last, depth=512):
    rows, half = got.shape
    width = hidden.shape[1]
    steps = half // depth
    experts = last.shape[0]
    tiles = width // DH
    packed = (experts, tiles * CAP, DH)

    def full(shape):
        return pl.BlockSpec(shape, lambda step, core_ref: (0,) * len(shape))

    def w_map(step, core_ref):
        return (1 - core_ref[0]) * steps + jnp.minimum(step, steps - 1), 0

    return pl.pallas_call(
        functools.partial(project_kernel, steps=steps),
        grid_spec=pltpu.PrefetchScalarGridSpec(
            num_scalar_prefetch=1,
            grid=(steps + packed[1] // STRIPE,),
            in_specs=[
                full((rows, width)),
                full((rows, half)),
                pl.BlockSpec((depth, width), w_map),
                full((rows, width)),
                full((1, width)),
                full(pick.shape),
                full(last.shape),
            ],
            out_specs=[
                full((rows, width)),
                full((rows, width)),
                pl.BlockSpec(
                    (experts, STRIPE, DH),
                    lambda step, core_ref: (0, jnp.maximum(step - steps, 0), 0),
                ),
            ],
            scratch_shapes=[
                pltpu.VMEM((rows, width), F32),
                pltpu.VMEM((experts, tiles, DH), F32),
            ],
        ),
        out_shape=[
            jax.ShapeDtypeStruct((rows, width), BF16),
            jax.ShapeDtypeStruct((rows, width), BF16),
            jax.ShapeDtypeStruct(packed, BF16),
        ],
        compiler_params=params("arbitrary"),
        name="project",
    )(core, part, got, w_out, hidden, gain, pick, last)


def expert_kernel(
    in_ref, gate_ref, up_ref, down_ref, out_ref, rows_ref, act_ref, over_ref, *, steps, up_steps
):
    step = pl.program_id(0)
    tile = gate_ref.shape[1]
    sources = in_ref.shape[0]
    main_rows = sources * MAIN
    tiles = gate_ref.shape[0] // DH
    stripe = in_ref.shape[1] // MAIN
    third = sources * CAP // 3

    for index in range(steps):

        @pl.when(step == index)
        def _(index=index):
            first = index * stripe
            held = min(stripe, tiles - first)
            for place in range(held):
                columns = pl.ds((first + place) * DH, DH)
                rows_ref[:main_rows, columns] = in_ref[
                    :, place * MAIN : (place + 1) * MAIN, :
                ].reshape(main_rows, DH)
            if held < stripe:
                over_ref[...] = in_ref[:, held * MAIN :, :].astype(F32)
                for place in range(tiles):
                    columns = pl.ds(place * DH, DH)
                    rows_ref[main_rows:, columns] = over_ref[:, place, :].astype(BF16)

    for index in range(up_steps):

        @pl.when(step == steps + index)
        def _(index=index):
            for start in range(0, 3 * third, third):
                rows = rows_ref[start : start + third, :]
                gate = jnp.dot(rows, gate_ref[...], preferred_element_type=F32)
                up = jnp.dot(rows, up_ref[...], preferred_element_type=F32)
                act = gate / (1.0 + jnp.exp(-gate)) * up
                act_ref[start : start + third, index * tile : (index + 1) * tile] = act.astype(BF16)

    for index in range(steps):

        @pl.when(step == steps + up_steps + index)
        def _(index=index):
            first = index * stripe
            held = min(stripe, tiles - first)
            for start in range(0, 3 * third, third):
                rows = jnp.dot(
                    act_ref[start : start + third, :],
                    down_ref[:, : held * DH],
                    preferred_element_type=F32,
                )
                some = min(third, main_rows - start)
                out_ref[start // MAIN : (start + some) // MAIN, : held * MAIN, :] = tiled_rows(
                    rows[:some]
                )
                if some < third:
                    for place in range(held):
                        over_ref[:, first + place, :] = rows[some:, place * DH : (place + 1) * DH]
            if held < stripe:
                out_ref[:, held * MAIN :, :] = over_ref[...].astype(BF16)


def experts_of(packed, w_gate, w_up, w_down):
    sources = packed.shape[0]
    width, hidden_units = w_gate.shape
    tile = 256
    steps = packed.shape[1] // STRIPE
    up_steps = hidden_units // tile
    rows = sources * CAP

    def out_step(step):
        return jnp.maximum(step - steps - up_steps, 0)

    def up_map(step):
        return 0, jnp.clip(step - steps, 0, up_steps - 1)

    return pl.pallas_call(
        functools.partial(expert_kernel, steps=steps, up_steps=up_steps),
        grid=(2 * steps + up_steps,),
        in_specs=[
            pl.BlockSpec((sources, STRIPE, DH), lambda step: (0, jnp.minimum(step, steps - 1), 0)),
            pl.BlockSpec((width, tile), up_map),
            pl.BlockSpec((width, tile), up_map),
            pl.BlockSpec((hidden_units, STRIPE // MAIN * DH), lambda step: (0, out_step(step))),
        ],
        out_specs=pl.BlockSpec((sources, STRIPE, DH), lambda step: (0, out_step(step), 0)),
        out_shape=jax.ShapeDtypeStruct(packed.shape, BF16),
        scratch_shapes=[
            pltpu.VMEM((rows, width), BF16),
            pltpu.VMEM((rows, hidden_units), BF16),
            pltpu.VMEM((sources, width // DH, DH), F32),
        ],
        compiler_params=params("arbitrary"),
        name="experts_of",
    )(packed, w_gate, w_up, w_down)


def combine_kernel(
    mix_ref, last_ref, in_ref, in_over_ref, h1_ref, out_ref, over_ref, *, tiles
):
    step = pl.program_id(0)
    stripe = in_ref.shape[1] // MAIN

    @pl.when(step == 0)
    def _():
        over_ref[...] = in_over_ref[...].astype(F32)

    for index in range(pl.cdiv(tiles, stripe)):

        @pl.when(step == index)
        def _(index=index):
            first = index * stripe
            held = min(stripe, tiles - first)
            rows = jnp.concatenate(
                [
                    in_ref[:, p * MAIN : (p + 1) * MAIN, :].reshape(BLOCK * MAIN, DH)
                    for p in range(held)
                ],
                axis=1,
            )
            extra = jnp.concatenate(
                [over_ref[:, first + p, :].astype(BF16) for p in range(held)], axis=1
            )
            total = jnp.dot(mix_ref[...], rows, preferred_element_type=F32)
            total = total + jnp.dot(last_ref[...], extra, preferred_element_type=F32)
            columns = slice(first * DH, (first + held) * DH)
            out_ref[:, columns] = (total + h1_ref[:, columns].astype(F32)).astype(BF16)


def combine(mix, last, packed, h1):
    rows, width = h1.shape
    experts = packed.shape[0]
    tiles = width // DH

    def whole(shape):
        return pl.BlockSpec(shape, lambda step: (0,) * len(shape))

    return pl.pallas_call(
        functools.partial(combine_kernel, tiles=tiles),
        grid=(packed.shape[1] // STRIPE,),
        in_specs=[
            whole(mix.shape),
            whole(last.shape),
            pl.BlockSpec((experts, STRIPE, DH), lambda step: (0, step, 0)),
            pl.BlockSpec((experts, tiles, DH), lambda step: (0, MAIN, 0)),
            whole(h1.shape),
        ],
        out_specs=whole(h1.shape),
        out_shape=jax.ShapeDtypeStruct((rows, width), BF16),
        scratch_shapes=[pltpu.VMEM((experts, tiles, DH), F32)],
        compiler_params=params("arbitrary"),
        name="combine",
    )(mix, last, packed, packed, h1)


def exchange(packed):
    return lax.all_to_all(packed, TORUS, split_axis=0, concat_axis=0, tiled=True)


def ring_near(piece, axes):
    left = lax.ppermute(piece, axes, [(i, (i + 1) % 4) for i in range(4)])
    right = lax.ppermute(piece, axes, [(i, (i + 3) % 4) for i in range(4)])
    return left, right


def ring_far(left, right, axes):
    half = left.shape[0] // 2
    low = lax.ppermute(left[:half], axes, [(i, (i + 1) % 4) for i in range(4)])
    high = lax.ppermute(right[half:], axes, [(i, (i + 3) % 4) for i in range(4)])
    return low, high


def ring_gather(piece, axes):
    left, right = ring_near(piece, axes)
    far = lax.ppermute(piece, axes, [(i, (i + 2) % 4) for i in range(4)])
    return jnp.concatenate([piece, left, right, far], axis=0)


def local(
    hidden, queries, keys, values, w_out, norm_gain, w_router, expert_ids, w_gate, w_up, w_down
):
    rows = hidden.shape[0]
    device = lax.axis_index(AXES)
    core = lax.axis_index("c")
    positions = device * rows + jnp.arange(rows, dtype=jnp.int32)
    cos_t, sin_t = yarn_tables(positions, DH)
    core_arr = core.reshape(1).astype(jnp.int32)
    keep, give, keep_kv, give_kv = rotate_all(core_arr, queries, keys, values, cos_t, sin_t)
    mirror = [(i, BLOCKS - 1 - i) for i in range(BLOCKS)]
    taken = lax.ppermute(give, AXES, mirror)
    other_kv = lax.ppermute(give_kv, ("c",), [(0, 1), (1, 0)])
    is_low = core == 0
    chip = jnp.concatenate(
        [jnp.where(is_low, keep_kv, other_kv), jnp.where(is_low, other_kv, keep_kv)], axis=0
    )
    row = lax.all_gather(chip, ("x",), axis=0)
    low = row[:, :rows].reshape(UNIT * rows, 2 * DH)
    high = row[:, rows:].reshape(UNIT * rows, 2 * DH)
    low = ring_gather(low, RING_Y)
    high = ring_gather(high, RING_Z)
    low_near = ring_near(low, RING_Z)
    high_near = ring_near(high, RING_Y)
    low_far = ring_far(*low_near, RING_Z)
    high_far = ring_far(*high_near, RING_Y)

    def units(order):
        return [(outer, inner, 0) for outer in order for inner in OFFSETS] + [
            (inner, outer, 1) for outer in order for inner in OFFSETS
        ]

    meta = jnp.stack(
        [BLOCKS - 1 - device, device, lax.axis_index(RING_Z), lax.axis_index(RING_Y)]
    ).astype(jnp.int32)
    state = attend(meta, units((0,)), taken, keep, [low, high])
    state = attend(meta, units((-1, 1)), taken, keep, [*low_near, *high_near], state=state)
    theirs, own = attend(
        meta, units((2,)), taken, keep, [*low_far, *high_far], state=state, last=True
    )
    got = lax.ppermute(theirs, AXES, mirror)
    part = project_own(core_arr, own, w_out)
    slot, pick, last = plan(torus_place(expert_ids.T))
    h1, hn, packed = project(
        core_arr, part, got, w_out, hidden, norm_gain[None, :], pick, last
    )
    arrived = exchange(packed)
    mix, last = routes(hn, w_router, expert_ids.T, slot)
    returned = exchange(experts_of(arrived, w_gate[0], w_up[0], w_down[0]))
    return combine(mix, last, returned, h1)


def solution(mesh):
    torus = Mesh(mesh.devices.reshape(2, 4, 2, 2, 4), AXES)
    split = P(AXES, None)
    experts = P(AXES, None, None)
    in_specs = (
        split, split, split, split, P(), P(), P(), split, experts, experts, experts,
    )
    return jax.shard_map(local, mesh=torus, in_specs=in_specs, out_specs=split, check_vma=False)
```

```python
import functools
import math

import jax
import jax.numpy as jnp
from jax import lax
from jax.experimental import pallas as pl
from jax.experimental.pallas import tpu as pltpu
from jax.sharding import Mesh, PartitionSpec as P


DH = 128
TOP = 8
CAP = 9
MAIN = 8
STRIPE = 48
BLOCK = 128
BLOCKS = 128
UNIT = 4
TILE_HEADS = 4
AXES = ("zh", "y", "c", "zl", "x")
TORUS = ("zh", "zl", "y", "x", "c")
RING_Z = ("zh", "zl")
RING_Y = ("y",)
OFFSETS = (0, -1, 1, 2)

rope_base = 1000000.0
yarn_factor = 4.0
orig_len = 32768.0
beta_fast = 32.0
beta_slow = 1.0
mscale_yarn = 0.1 * math.log(4.0) + 1.0


F32 = jnp.float32
BF16 = jnp.bfloat16
VMEM_LIMIT = 60 * 1024 * 1024


def params(*semantics):
    return pltpu.CompilerParams(
        dimension_semantics=semantics, vmem_limit_bytes=VMEM_LIMIT
    )


def yarn_tables(positions, head_size):
    half_size = head_size // 2
    index_f = jnp.arange(half_size, dtype=jnp.float32)
    pos_freq = rope_base ** (2.0 * index_f / head_size)
    inv_extra = 1.0 / pos_freq
    inv_inter = 1.0 / (yarn_factor * pos_freq)
    low_dim = max(
        math.floor(
            head_size
            * math.log(orig_len / (beta_fast * 2.0 * math.pi))
            / (2.0 * math.log(rope_base))
        ),
        0,
    )
    high_dim = min(
        math.ceil(
            head_size
            * math.log(orig_len / (beta_slow * 2.0 * math.pi))
            / (2.0 * math.log(rope_base))
        ),
        head_size - 1,
    )
    ramp_part = jnp.clip((index_f - low_dim) / max(high_dim - low_dim, 0.001), 0.0, 1.0)
    extra_part = 1.0 - ramp_part
    inverse = inv_inter * (1.0 - extra_part) + inv_extra * extra_part
    angles = positions.astype(jnp.float32)[:, None] * inverse[None, :]
    cos_half = jnp.cos(angles) * mscale_yarn
    sin_half = jnp.sin(angles) * mscale_yarn
    return (
        jnp.concatenate([cos_half, cos_half], axis=-1),
        jnp.concatenate([-sin_half, sin_half], axis=-1),
    )


def rotate_kernel(
    core_ref, q_ref, k_ref, v_ref, cos_ref, sin_ref, keep_ref, give_ref, keep_kv_ref, give_kv_ref
):
    core = core_ref[0]
    cos_t = cos_ref[...]
    sin_t = sin_ref[...]

    def rotated(part):
        value = part.astype(F32)
        return (value * cos_t + pltpu.roll(value, DH // 2, 1) * sin_t).astype(BF16)

    half = keep_ref.shape[1]
    for q_out, kv_out, which in (
        (keep_ref, keep_kv_ref, core),
        (give_ref, give_kv_ref, 1 - core),
    ):
        head_span = pl.ds(pl.multiple_of(which * DH, DH), DH)
        kv_out[:, :DH] = rotated(k_ref[:, head_span])
        kv_out[:, DH:] = v_ref[:, head_span]
        for head in range(half // DH):
            source = pl.ds(pl.multiple_of(which * half + head * DH, DH), DH)
            q_out[:, pl.ds(head * DH, DH)] = rotated(q_ref[:, source])


def rotate_all(core, queries, keys, values, cos_t, sin_t):
    rows, width = queries.shape
    vmem = pl.BlockSpec(memory_space=pltpu.VMEM)
    return pl.pallas_call(
        rotate_kernel,
        in_specs=[pl.BlockSpec(memory_space=pltpu.SMEM)] + [vmem] * 5,
        out_specs=[vmem] * 4,
        out_shape=[jax.ShapeDtypeStruct((rows, width // 2), BF16)] * 2
        + [jax.ShapeDtypeStruct((rows, 2 * DH), BF16)] * 2,
        compiler_params=params(),
        name="rotate_all",
    )(core, queries, keys, values, cos_t, sin_t)


def first_block(z, y, c):
    return z // 2 * 64 + y * 16 + c * 8 + z % 2 * 4


def attend_kernel(meta_ref, theirs_ref, own_ref, *refs, units, pieces, heads, tile_heads, first, last):
    piece_refs, refs = refs[:pieces], refs[pieces:]
    if not first:
        state_in, refs = refs[:3], refs[3:]
    if last:
        out_refs, refs = refs[:2], refs[2:]
    else:
        state_out, refs = refs[:3], refs[3:]
    state, refs = refs[:3], refs[3:]
    kv_ref, q_ref, base_ref, list_ref, tail_ref, kv_sem, q_sem, in_sem, out_sem = refs
    max_ref, sum_ref, acc_ref = state
    unit_rows = UNIT * BLOCK
    half_rows = heads * BLOCK

    def half_copies(which, sources, targets, sems):
        span = pl.ds(pl.multiple_of(which * half_rows, half_rows), half_rows)
        return [
            pltpu.make_async_copy(source.at[span, :], target.at[span, :], sems.at[which, index])
            for index, (source, target) in enumerate(zip(sources, targets))
        ]

    copies = [
        pltpu.make_async_copy(theirs_ref, q_ref.at[0], q_sem.at[0]),
        pltpu.make_async_copy(own_ref, q_ref.at[1], q_sem.at[1]),
    ]
    place = 0
    for index, piece in enumerate(piece_refs):
        size = piece.shape[0]
        copies.append(
            pltpu.make_async_copy(piece, kv_ref.at[pl.ds(place, size), :], kv_sem.at[index])
        )
        place += size
    for copy in copies:
        copy.start()
    if first:
        max_ref[...] = jnp.full_like(max_ref, -1e30)
        sum_ref[...] = jnp.zeros_like(sum_ref)
        acc_ref[...] = jnp.zeros_like(acc_ref)
    else:
        for which in range(2):
            for copy in half_copies(which, state_in, state, in_sem):
                copy.start()
    for index, (z_off, y_off, c) in enumerate(units):
        base_ref[index] = first_block((meta_ref[2] + z_off) % 4, (meta_ref[3] + y_off) % 4, c)
    for copy in copies:
        copy.wait()

    factor = math.log2(math.e) / math.sqrt(DH)
    rows = tile_heads * BLOCK
    parts = heads // tile_heads

    @pl.loop(0, 2)
    def _(which):
        block = meta_ref[which]
        if not first:
            for copy in half_copies(which, state_in, state, in_sem):
                copy.wait()

        def update(taken, masked):
            keys_len = len(taken) * unit_rows
            starts = [pl.multiple_of(unit * unit_rows, unit_rows) for unit in taken]
            keys = jnp.concatenate([kv_ref[pl.ds(s, unit_rows), :DH] for s in starts], axis=0)
            vals = jnp.concatenate([kv_ref[pl.ds(s, unit_rows), DH:] for s in starts], axis=0)
            if masked:
                shape = (BLOCK, unit_rows)
                row_token = lax.broadcasted_iota(jnp.int32, shape, 0)
                key_token = lax.broadcasted_iota(jnp.int32, shape, 1)
                ahead = (base_ref[taken[0]] - block) * BLOCK
                allowed = key_token + ahead <= row_token

            def scores_of(part):
                query = jnp.concatenate(
                    [
                        q_ref[which, :, pl.ds((part * tile_heads + h) * DH, DH)]
                        for h in range(tile_heads)
                    ],
                    axis=0,
                )
                scores = lax.dot_general(
                    query, keys, (((1,), (1,)), ((), ())), preferred_element_type=F32
                )
                if masked:
                    scores = jnp.where(
                        allowed[None], scores.reshape(tile_heads, BLOCK, keys_len), -1e30
                    ).reshape(rows, keys_len)
                return scores

            def absorb(part, scores):
                start = pl.multiple_of((which * heads + part * tile_heads) * BLOCK, BLOCK)
                span = pl.ds(start, rows)
                old_max = max_ref[span, :]
                new_max = jnp.maximum(old_max, jnp.max(scores, axis=1, keepdims=True))
                decay = jnp.exp2((old_max - new_max) * factor)
                lane_sum = sum_ref[span, :] * decay
                weights = []
                for column in range(keys_len // DH):
                    some = scores[:, column * DH : (column + 1) * DH]
                    piece = jnp.exp2((some - new_max) * factor)
                    lane_sum = lane_sum + piece
                    weights.append(piece.astype(BF16))
                sum_ref[span, :] = lane_sum
                max_ref[span, :] = new_max
                added = jnp.dot(jnp.concatenate(weights, axis=1), vals, preferred_element_type=F32)
                acc_ref[span, :] = acc_ref[span, :] * decay + added

            scores = scores_of(0)
            for part in range(parts):
                later = scores_of(part + 1) if part + 1 < parts else None
                absorb(part, scores)
                scores = later

        count = jnp.int32(0)
        tail = jnp.int32(0)
        for unit in range(len(units)):
            base = base_ref[unit]
            list_ref[count] = unit
            tail_ref[tail] = unit
            count = count + jnp.where(base + UNIT <= block, 1, 0)
            tail = tail + jnp.where(jnp.logical_and(base <= block, block < base + UNIT), 1, 0)
        pairs = count // 2
        tail_ref[tail] = list_ref[jnp.maximum(count - 1, 0)]
        tail = tail + count - 2 * pairs

        @pl.loop(0, pairs)
        def _(step):
            update([list_ref[2 * step], list_ref[2 * step + 1]], False)

        @pl.loop(0, tail)
        def _(step):
            update([tail_ref[step]], True)

        if not last:
            for copy in half_copies(which, state, state_out, out_sem):
                copy.start()

    if not last:
        for which in range(2):
            for copy in half_copies(which, state, state_out, out_sem):
                copy.wait()
    if last:
        for head in range(2 * heads):
            span = pl.ds(head * BLOCK, BLOCK)
            total = jnp.sum(sum_ref[span, :], axis=1, keepdims=True)
            out_refs[head // heads][:, pl.ds(head % heads * DH, DH)] = (
                acc_ref[span, :] / total
            ).astype(BF16)


def attend(meta, units, theirs, own, pieces, state=None, last=False, tile_heads=TILE_HEADS):
    rows, width = own.shape
    heads = width // DH
    smem = pl.BlockSpec(memory_space=pltpu.SMEM)
    vmem = pl.BlockSpec(memory_space=pltpu.VMEM)
    anywhere = pl.BlockSpec(memory_space=pl.ANY)
    states = [(2 * heads * rows, DH)] * 3
    scratch = [pltpu.VMEM(shape, F32) for shape in states] + [
        pltpu.VMEM((len(units) * UNIT * BLOCK, 2 * DH), BF16),
        pltpu.VMEM((2, rows, width), BF16),
        pltpu.SMEM((len(units),), jnp.int32),
        pltpu.SMEM((len(units) + 1,), jnp.int32),
        pltpu.SMEM((len(units) + 2,), jnp.int32),
        pltpu.SemaphoreType.DMA((len(pieces),)),
        pltpu.SemaphoreType.DMA((2,)),
        pltpu.SemaphoreType.DMA((2, 3)),
        pltpu.SemaphoreType.DMA((2, 3)),
    ]
    if last:
        out_shape = [jax.ShapeDtypeStruct((rows, width), BF16)] * 2
    else:
        out_shape = [jax.ShapeDtypeStruct(shape, F32) for shape in states]
    state = [] if state is None else list(state)
    kernel = functools.partial(
        attend_kernel,
        units=units,
        pieces=len(pieces),
        heads=heads,
        tile_heads=tile_heads,
        first=not state,
        last=last,
    )
    keys_seen = len(units) * UNIT * BLOCK
    return pl.pallas_call(
        kernel,
        in_specs=[smem] + [anywhere] * (2 + len(pieces) + len(state)),
        out_specs=[vmem if last else anywhere] * len(out_shape),
        out_shape=out_shape,
        scratch_shapes=scratch,
        compiler_params=params(),
        cost_estimate=pl.CostEstimate(
            flops=4 * keys_seen * heads * rows * DH,
            bytes_accessed=keys_seen * 4 * DH,
            transcendentals=keys_seen * heads * rows,
        ),
        name="attend_last" if last else "attend_more" if state else "attend_first",
    )(meta, theirs, own, *pieces, *state)


def slots_of(ids_ref):
    shape = (BLOCK, BLOCK)
    expert = lax.broadcasted_iota(jnp.int32, shape, 0)
    named = jnp.zeros(shape, F32)
    for k in range(TOP):
        named = named + jnp.where(ids_ref[k : k + 1, :] == expert, 1.0, 0.0)
    earlier = jnp.where(
        lax.broadcasted_iota(jnp.int32, shape, 0) < lax.broadcasted_iota(jnp.int32, shape, 1),
        1.0,
        0.0,
    )
    counts = jnp.dot(named.astype(BF16), earlier.astype(BF16), preferred_element_type=F32)
    return named, jnp.where(named > 0.0, counts, -1.0)


def own_kernel(core_ref, own_ref, w_ref, out_ref):
    @pl.when(pl.program_id(0) == 0)
    def _():
        out_ref[...] = jnp.zeros_like(out_ref)

    depth = w_ref.shape[0]
    column = pl.ds(pl.multiple_of(pl.program_id(0) * depth, depth), depth)
    out_ref[...] += jnp.dot(own_ref[:, column], w_ref[...], preferred_element_type=F32)


def project_own(core, own, w_out, depth=512):
    rows, half = own.shape
    width = w_out.shape[1]
    steps = half // depth
    return pl.pallas_call(
        own_kernel,
        grid_spec=pltpu.PrefetchScalarGridSpec(
            num_scalar_prefetch=1,
            grid=(steps,),
            in_specs=[
                pl.BlockSpec((rows, half), lambda step, core_ref: (0, 0)),
                pl.BlockSpec((depth, width), lambda step, core_ref: (core_ref[0] * steps + step, 0)),
            ],
            out_specs=pl.BlockSpec((rows, width), lambda step, core_ref: (0, 0)),
        ),
        out_shape=jax.ShapeDtypeStruct((rows, width), F32),
        compiler_params=params("arbitrary"),
        cost_estimate=pl.CostEstimate(
            flops=2 * rows * half * width, bytes_accessed=2 * half * width, transcendentals=0
        ),
        name="project_own",
    )(core, own, w_out)


def torus_place(expert):
    zh, y, c = expert // 64, expert // 16 % 4, expert // 8 % 2
    zl, x = expert // 4 % 2, expert % 4
    return zh * 64 + zl * 32 + y * 8 + x * 2 + c


def plan_kernel(ids_ref, slot_ref, pick_ref, last_ref):
    slot = slots_of(ids_ref)[1]
    slot_ref[...] = slot
    wanted = lax.broadcasted_iota(jnp.int32, (BLOCK, MAIN, BLOCK), 1).astype(F32)
    pick = jnp.where(slot[:, None, :] == wanted, 1.0, 0.0).reshape(BLOCK * MAIN, BLOCK)
    pick_ref[...] = pick.astype(BF16)
    last_ref[...] = jnp.where(slot == float(MAIN), 1.0, 0.0).astype(BF16)


def plan(places_t):
    rows = places_t.shape[1]
    vmem = pl.BlockSpec(memory_space=pltpu.VMEM)
    return pl.pallas_call(
        plan_kernel,
        in_specs=[vmem],
        out_specs=[vmem] * 3,
        out_shape=[
            jax.ShapeDtypeStruct((BLOCKS, rows), F32),
            jax.ShapeDtypeStruct((BLOCKS * MAIN, rows), BF16),
            jax.ShapeDtypeStruct((BLOCKS, rows), BF16),
        ],
        compiler_params=params(),
        name="plan",
    )(places_t)


def routes_kernel(hn_ref, router_ref, ids_ref, slot_ref, mix_ref, last_ref):
    logits = jnp.dot(hn_ref[...], router_ref[...], preferred_element_type=F32)
    named = slots_of(ids_ref)[0]
    raised = jnp.where(named > 0.0, jnp.exp(jnp.transpose(logits)), 0.0)
    by_expert = (raised / jnp.sum(raised, axis=0, keepdims=True)).astype(BF16)
    shape = (BLOCK, BLOCK)
    place = torus_place(lax.broadcasted_iota(jnp.int32, shape, 1))
    order = jnp.where(place == lax.broadcasted_iota(jnp.int32, shape, 0), 1.0, 0.0)
    route = jnp.dot(order.astype(BF16), by_expert, preferred_element_type=F32)
    slot = slot_ref[...]
    wanted = lax.broadcasted_iota(jnp.int32, (BLOCK, MAIN, BLOCK), 1).astype(F32)
    mix = jnp.where(slot[:, None, :] == wanted, route[:, None, :], 0.0)
    mix_ref[...] = jnp.transpose(mix.reshape(BLOCK * MAIN, BLOCK).astype(BF16))
    last_ref[...] = jnp.transpose(jnp.where(slot == float(MAIN), route, 0.0)).astype(BF16)


def routes(hn, w_router, ids_t, slot):
    rows = hn.shape[0]
    vmem = pl.BlockSpec(memory_space=pltpu.VMEM)
    return pl.pallas_call(
        routes_kernel,
        in_specs=[vmem] * 4,
        out_specs=[vmem] * 2,
        out_shape=[
            jax.ShapeDtypeStruct((rows, BLOCKS * MAIN), BF16),
            jax.ShapeDtypeStruct((rows, BLOCKS), BF16),
        ],
        compiler_params=params(),
        name="routes",
    )(hn, w_router, ids_t, slot)


def project_kernel(
    core_ref, part_ref, got_ref, w_ref, hidden_ref, gain_ref, pick_ref, last_ref,
    h1_ref, hn_ref, send_ref, acc_ref, over_ref, *, steps,
):
    step = pl.program_id(0)
    depth = w_ref.shape[0]
    tiles = hn_ref.shape[1] // DH

    @pl.when(step == 0)
    def _():
        acc_ref[...] = part_ref[...] + hidden_ref[...].astype(F32)

    @pl.when(step < steps)
    def _():
        column = pl.ds(pl.multiple_of(step * depth, depth), depth)
        acc_ref[...] += jnp.dot(got_ref[:, column], w_ref[...], preferred_element_type=F32)

    @pl.when(step == steps - 1)
    def _():
        h1 = acc_ref[...].astype(BF16)
        h1_ref[...] = h1
        h1_f = h1.astype(F32)
        mean = jnp.mean(h1_f * h1_f, axis=-1, keepdims=True)
        hn = (h1_f / jnp.sqrt(mean + 1e-06) * gain_ref[...]).astype(BF16)
        hn_ref[...] = hn
        for tile in range(tiles):
            part = hn[:, tile * DH : (tile + 1) * DH]
            over_ref[:, tile, :] = jnp.dot(last_ref[...], part, preferred_element_type=F32)

    stripe = send_ref.shape[1] // MAIN
    for index in range(pl.cdiv(tiles, stripe)):

        @pl.when(step == steps + index)
        def _(index=index):
            first = index * stripe
            held = min(stripe, tiles - first)
            columns = hn_ref[:, first * DH : (first + held) * DH]
            rows = jnp.dot(pick_ref[...], columns, preferred_element_type=F32)
            send_ref[:, : held * MAIN, :] = tiled_rows(rows)
            if held < stripe:
                send_ref[:, held * MAIN :, :] = over_ref[...].astype(BF16)


def tiled_rows(rows):
    sources = rows.shape[0] // MAIN
    pieces = [
        rows[:, tile * DH : (tile + 1) * DH].reshape(sources, MAIN, DH)
        for tile in range(rows.shape[1] // DH)
    ]
    return jnp.concatenate(pieces, axis=1).astype(BF16)


def project(core, part, got, w_out, hidden, gain, pick, last, depth=512):
    rows, half = got.shape
    width = hidden.shape[1]
    steps = half // depth
    experts = last.shape[0]
    tiles = width // DH
    packed = (experts, tiles * CAP, DH)

    def full(shape):
        return pl.BlockSpec(shape, lambda step, core_ref: (0,) * len(shape))

    def w_map(step, core_ref):
        return (1 - core_ref[0]) * steps + jnp.minimum(step, steps - 1), 0

    return pl.pallas_call(
        functools.partial(project_kernel, steps=steps),
        grid_spec=pltpu.PrefetchScalarGridSpec(
            num_scalar_prefetch=1,
            grid=(steps + packed[1] // STRIPE,),
            in_specs=[
                full((rows, width)),
                full((rows, half)),
                pl.BlockSpec((depth, width), w_map),
                full((rows, width)),
                full((1, width)),
                full(pick.shape),
                full(last.shape),
            ],
            out_specs=[
                full((rows, width)),
                full((rows, width)),
                pl.BlockSpec(
                    (experts, STRIPE, DH),
                    lambda step, core_ref: (0, jnp.maximum(step - steps, 0), 0),
                ),
            ],
            scratch_shapes=[
                pltpu.VMEM((rows, width), F32),
                pltpu.VMEM((experts, tiles, DH), F32),
            ],
        ),
        out_shape=[
            jax.ShapeDtypeStruct((rows, width), BF16),
            jax.ShapeDtypeStruct((rows, width), BF16),
            jax.ShapeDtypeStruct(packed, BF16),
        ],
        compiler_params=params("arbitrary"),
        name="project",
    )(core, part, got, w_out, hidden, gain, pick, last)


def expert_kernel(
    in_ref, gate_ref, up_ref, down_ref, out_ref, rows_ref, act_ref, over_ref, *, steps, up_steps
):
    step = pl.program_id(0)
    tile = gate_ref.shape[1]
    sources = in_ref.shape[0]
    main_rows = sources * MAIN
    tiles = gate_ref.shape[0] // DH
    stripe = in_ref.shape[1] // MAIN
    third = sources * CAP // 3

    for index in range(steps):

        @pl.when(step == index)
        def _(index=index):
            first = index * stripe
            held = min(stripe, tiles - first)
            for place in range(held):
                columns = pl.ds((first + place) * DH, DH)
                rows_ref[:main_rows, columns] = in_ref[
                    :, place * MAIN : (place + 1) * MAIN, :
                ].reshape(main_rows, DH)
            if held < stripe:
                over_ref[...] = in_ref[:, held * MAIN :, :].astype(F32)
                for place in range(tiles):
                    columns = pl.ds(place * DH, DH)
                    rows_ref[main_rows:, columns] = over_ref[:, place, :].astype(BF16)

    for index in range(up_steps):

        @pl.when(step == steps + index)
        def _(index=index):
            for start in range(0, 3 * third, third):
                rows = rows_ref[start : start + third, :]
                gate = jnp.dot(rows, gate_ref[...], preferred_element_type=F32)
                up = jnp.dot(rows, up_ref[...], preferred_element_type=F32)
                act = gate / (1.0 + jnp.exp(-gate)) * up
                act_ref[start : start + third, index * tile : (index + 1) * tile] = act.astype(BF16)

    for index in range(steps):

        @pl.when(step == steps + up_steps + index)
        def _(index=index):
            first = index * stripe
            held = min(stripe, tiles - first)
            for start in range(0, 3 * third, third):
                rows = jnp.dot(
                    act_ref[start : start + third, :],
                    down_ref[:, : held * DH],
                    preferred_element_type=F32,
                )
                some = min(third, main_rows - start)
                out_ref[start // MAIN : (start + some) // MAIN, : held * MAIN, :] = tiled_rows(
                    rows[:some]
                )
                if some < third:
                    for place in range(held):
                        over_ref[:, first + place, :] = rows[some:, place * DH : (place + 1) * DH]
            if held < stripe:
                out_ref[:, held * MAIN :, :] = over_ref[...].astype(BF16)


def experts_of(packed, w_gate, w_up, w_down):
    sources = packed.shape[0]
    width, hidden_units = w_gate.shape
    tile = 256
    steps = packed.shape[1] // STRIPE
    up_steps = hidden_units // tile
    rows = sources * CAP

    def out_step(step):
        return jnp.maximum(step - steps - up_steps, 0)

    def up_map(step):
        return 0, jnp.clip(step - steps, 0, up_steps - 1)

    return pl.pallas_call(
        functools.partial(expert_kernel, steps=steps, up_steps=up_steps),
        grid=(2 * steps + up_steps,),
        in_specs=[
            pl.BlockSpec((sources, STRIPE, DH), lambda step: (0, jnp.minimum(step, steps - 1), 0)),
            pl.BlockSpec((width, tile), up_map),
            pl.BlockSpec((width, tile), up_map),
            pl.BlockSpec((hidden_units, STRIPE // MAIN * DH), lambda step: (0, out_step(step))),
        ],
        out_specs=pl.BlockSpec((sources, STRIPE, DH), lambda step: (0, out_step(step), 0)),
        out_shape=jax.ShapeDtypeStruct(packed.shape, BF16),
        scratch_shapes=[
            pltpu.VMEM((rows, width), BF16),
            pltpu.VMEM((rows, hidden_units), BF16),
            pltpu.VMEM((sources, width // DH, DH), F32),
        ],
        compiler_params=params("arbitrary"),
        name="experts_of",
    )(packed, w_gate, w_up, w_down)


def combine_kernel(
    mix_ref, last_ref, in_ref, in_over_ref, h1_ref, out_ref, over_ref, *, tiles
):
    step = pl.program_id(0)
    stripe = in_ref.shape[1] // MAIN

    @pl.when(step == 0)
    def _():
        over_ref[...] = in_over_ref[...].astype(F32)

    for index in range(pl.cdiv(tiles, stripe)):

        @pl.when(step == index)
        def _(index=index):
            first = index * stripe
            held = min(stripe, tiles - first)
            rows = jnp.concatenate(
                [
                    in_ref[:, p * MAIN : (p + 1) * MAIN, :].reshape(BLOCK * MAIN, DH)
                    for p in range(held)
                ],
                axis=1,
            )
            extra = jnp.concatenate(
                [over_ref[:, first + p, :].astype(BF16) for p in range(held)], axis=1
            )
            total = jnp.dot(mix_ref[...], rows, preferred_element_type=F32)
            total = total + jnp.dot(last_ref[...], extra, preferred_element_type=F32)
            columns = slice(first * DH, (first + held) * DH)
            out_ref[:, columns] = (total + h1_ref[:, columns].astype(F32)).astype(BF16)


def combine(mix, last, packed, h1):
    rows, width = h1.shape
    experts = packed.shape[0]
    tiles = width // DH

    def whole(shape):
        return pl.BlockSpec(shape, lambda step: (0,) * len(shape))

    return pl.pallas_call(
        functools.partial(combine_kernel, tiles=tiles),
        grid=(packed.shape[1] // STRIPE,),
        in_specs=[
            whole(mix.shape),
            whole(last.shape),
            pl.BlockSpec((experts, STRIPE, DH), lambda step: (0, step, 0)),
            pl.BlockSpec((experts, tiles, DH), lambda step: (0, MAIN, 0)),
            whole(h1.shape),
        ],
        out_specs=whole(h1.shape),
        out_shape=jax.ShapeDtypeStruct((rows, width), BF16),
        scratch_shapes=[pltpu.VMEM((experts, tiles, DH), F32)],
        compiler_params=params("arbitrary"),
        name="combine",
    )(mix, last, packed, packed, h1)


def exchange(packed):
    return lax.all_to_all(packed, TORUS, split_axis=0, concat_axis=0, tiled=True)


def ring_near(piece, axes):
    left = lax.ppermute(piece, axes, [(i, (i + 1) % 4) for i in range(4)])
    right = lax.ppermute(piece, axes, [(i, (i + 3) % 4) for i in range(4)])
    return left, right


def ring_far(left, right, axes):
    half = left.shape[0] // 2
    low = lax.ppermute(left[:half], axes, [(i, (i + 1) % 4) for i in range(4)])
    high = lax.ppermute(right[half:], axes, [(i, (i + 3) % 4) for i in range(4)])
    return low, high


def ring_gather(piece, axes):
    left, right = ring_near(piece, axes)
    far = lax.ppermute(piece, axes, [(i, (i + 2) % 4) for i in range(4)])
    return jnp.concatenate([piece, left, right, far], axis=0)


def local(
    hidden, queries, keys, values, w_out, norm_gain, w_router, expert_ids, w_gate, w_up, w_down
):
    rows = hidden.shape[0]
    device = lax.axis_index(AXES)
    core = lax.axis_index("c")
    positions = device * rows + jnp.arange(rows, dtype=jnp.int32)
    cos_t, sin_t = yarn_tables(positions, DH)
    core_arr = core.reshape(1).astype(jnp.int32)
    keep, give, keep_kv, give_kv = rotate_all(core_arr, queries, keys, values, cos_t, sin_t)
    mirror = [(i, BLOCKS - 1 - i) for i in range(BLOCKS)]
    taken = lax.ppermute(give, AXES, mirror)
    other_kv = lax.ppermute(give_kv, ("c",), [(0, 1), (1, 0)])
    is_low = core == 0
    chip = jnp.concatenate(
        [jnp.where(is_low, keep_kv, other_kv), jnp.where(is_low, other_kv, keep_kv)], axis=0
    )
    row = lax.all_gather(chip, ("x",), axis=0)
    low = row[:, :rows].reshape(UNIT * rows, 2 * DH)
    high = row[:, rows:].reshape(UNIT * rows, 2 * DH)
    low = ring_gather(low, RING_Y)
    high = ring_gather(high, RING_Z)
    low_near = ring_near(low, RING_Z)
    high_near = ring_near(high, RING_Y)
    low_far = ring_far(*low_near, RING_Z)
    high_far = ring_far(*high_near, RING_Y)

    def units(order):
        return [(outer, inner, 0) for outer in order for inner in OFFSETS] + [
            (inner, outer, 1) for outer in order for inner in OFFSETS
        ]

    meta = jnp.stack(
        [BLOCKS - 1 - device, device, lax.axis_index(RING_Z), lax.axis_index(RING_Y)]
    ).astype(jnp.int32)
    state = attend(meta, units((0,)), taken, keep, [low, high])
    state = attend(meta, units((-1, 1)), taken, keep, [*low_near, *high_near], state=state)
    theirs, own = attend(
        meta, units((2,)), taken, keep, [*low_far, *high_far], state=state, last=True
    )
    got = lax.ppermute(theirs, AXES, mirror)
    part = project_own(core_arr, own, w_out)
    slot, pick, last = plan(torus_place(expert_ids.T))
    h1, hn, packed = project(
        core_arr, part, got, w_out, hidden, norm_gain[None, :], pick, last
    )
    arrived = exchange(packed)
    mix, last = routes(hn, w_router, expert_ids.T, slot)
    returned = exchange(experts_of(arrived, w_gate[0], w_up[0], w_down[0]))
    return combine(mix, last, returned, h1)


def solution(mesh):
    torus = Mesh(mesh.devices.reshape(2, 4, 2, 2, 4), AXES)
    split = P(AXES, None)
    experts = P(AXES, None, None)
    in_specs = (
        split, split, split, split, P(), P(), P(), split, experts, experts, experts,
    )
    return jax.shard_map(local, mesh=torus, in_specs=in_specs, out_specs=split, check_vma=False)
```

```python
import functools
import math

import jax
import jax.numpy as jnp
from jax import lax
from jax.experimental import pallas as pl
from jax.experimental.pallas import tpu as pltpu
from jax.sharding import Mesh, PartitionSpec as P


DH = 128
TOP = 8
CAP = 9
MAIN = 8
STRIPE = 48
BLOCK = 128
BLOCKS = 128
UNIT = 4
TILE_HEADS = 4
AXES = ("zh", "y", "c", "zl", "x")
TORUS = ("zh", "zl", "y", "x", "c")
RING_Z = ("zh", "zl")
RING_Y = ("y",)
OFFSETS = (0, -1, 1, 2)

rope_base = 1000000.0
yarn_factor = 4.0
orig_len = 32768.0
beta_fast = 32.0
beta_slow = 1.0
mscale_yarn = 0.1 * math.log(4.0) + 1.0


F32 = jnp.float32
BF16 = jnp.bfloat16
VMEM_LIMIT = 60 * 1024 * 1024


def params(*semantics):
    return pltpu.CompilerParams(
        dimension_semantics=semantics, vmem_limit_bytes=VMEM_LIMIT
    )


def yarn_tables(positions, head_size):
    half_size = head_size // 2
    index_f = jnp.arange(half_size, dtype=jnp.float32)
    pos_freq = rope_base ** (2.0 * index_f / head_size)
    inv_extra = 1.0 / pos_freq
    inv_inter = 1.0 / (yarn_factor * pos_freq)
    low_dim = max(
        math.floor(
            head_size
            * math.log(orig_len / (beta_fast * 2.0 * math.pi))
            / (2.0 * math.log(rope_base))
        ),
        0,
    )
    high_dim = min(
        math.ceil(
            head_size
            * math.log(orig_len / (beta_slow * 2.0 * math.pi))
            / (2.0 * math.log(rope_base))
        ),
        head_size - 1,
    )
    ramp_part = jnp.clip((index_f - low_dim) / max(high_dim - low_dim, 0.001), 0.0, 1.0)
    extra_part = 1.0 - ramp_part
    inverse = inv_inter * (1.0 - extra_part) + inv_extra * extra_part
    angles = positions.astype(jnp.float32)[:, None] * inverse[None, :]
    cos_half = jnp.cos(angles) * mscale_yarn
    sin_half = jnp.sin(angles) * mscale_yarn
    return (
        jnp.concatenate([cos_half, cos_half], axis=-1),
        jnp.concatenate([-sin_half, sin_half], axis=-1),
    )


def rotate_kernel(
    core_ref, q_ref, k_ref, v_ref, cos_ref, sin_ref, keep_ref, give_ref, keep_kv_ref, give_kv_ref
):
    core = core_ref[0]
    cos_t = cos_ref[...]
    sin_t = sin_ref[...]

    def rotated(part):
        value = part.astype(F32)
        return (value * cos_t + pltpu.roll(value, DH // 2, 1) * sin_t).astype(BF16)

    half = keep_ref.shape[1]
    for q_out, kv_out, which in (
        (keep_ref, keep_kv_ref, core),
        (give_ref, give_kv_ref, 1 - core),
    ):
        head_span = pl.ds(pl.multiple_of(which * DH, DH), DH)
        kv_out[:, :DH] = rotated(k_ref[:, head_span])
        kv_out[:, DH:] = v_ref[:, head_span]
        for head in range(half // DH):
            source = pl.ds(pl.multiple_of(which * half + head * DH, DH), DH)
            q_out[:, pl.ds(head * DH, DH)] = rotated(q_ref[:, source])


def rotate_all(core, queries, keys, values, cos_t, sin_t):
    rows, width = queries.shape
    vmem = pl.BlockSpec(memory_space=pltpu.VMEM)
    return pl.pallas_call(
        rotate_kernel,
        in_specs=[pl.BlockSpec(memory_space=pltpu.SMEM)] + [vmem] * 5,
        out_specs=[vmem] * 4,
        out_shape=[jax.ShapeDtypeStruct((rows, width // 2), BF16)] * 2
        + [jax.ShapeDtypeStruct((rows, 2 * DH), BF16)] * 2,
        compiler_params=params(),
        name="rotate_all",
    )(core, queries, keys, values, cos_t, sin_t)


def first_block(z, y, c):
    return z // 2 * 64 + y * 16 + c * 8 + z % 2 * 4


def attend_kernel(meta_ref, theirs_ref, own_ref, *refs, units, pieces, heads, tile_heads, first, last):
    piece_refs, refs = refs[:pieces], refs[pieces:]
    if not first:
        state_in, refs = refs[:3], refs[3:]
    if last:
        out_refs, refs = refs[:2], refs[2:]
    else:
        state_out, refs = refs[:3], refs[3:]
    state, refs = refs[:3], refs[3:]
    kv_ref, q_ref, base_ref, list_ref, tail_ref, kv_sem, q_sem, in_sem, out_sem = refs
    max_ref, sum_ref, acc_ref = state
    unit_rows = UNIT * BLOCK
    half_rows = heads * BLOCK

    def half_copies(which, sources, targets, sems):
        span = pl.ds(pl.multiple_of(which * half_rows, half_rows), half_rows)
        return [
            pltpu.make_async_copy(source.at[span, :], target.at[span, :], sems.at[which, index])
            for index, (source, target) in enumerate(zip(sources, targets))
        ]

    copies = [
        pltpu.make_async_copy(theirs_ref, q_ref.at[0], q_sem.at[0]),
        pltpu.make_async_copy(own_ref, q_ref.at[1], q_sem.at[1]),
    ]
    place = 0
    for index, piece in enumerate(piece_refs):
        size = piece.shape[0]
        copies.append(
            pltpu.make_async_copy(piece, kv_ref.at[pl.ds(place, size), :], kv_sem.at[index])
        )
        place += size
    for copy in copies:
        copy.start()
    if first:
        max_ref[...] = jnp.full_like(max_ref, -1e30)
        sum_ref[...] = jnp.zeros_like(sum_ref)
        acc_ref[...] = jnp.zeros_like(acc_ref)
    else:
        for which in range(2):
            for copy in half_copies(which, state_in, state, in_sem):
                copy.start()
    for index, (z_off, y_off, c) in enumerate(units):
        base_ref[index] = first_block((meta_ref[2] + z_off) % 4, (meta_ref[3] + y_off) % 4, c)
    for copy in copies:
        copy.wait()

    factor = math.log2(math.e) / math.sqrt(DH)
    rows = tile_heads * BLOCK
    parts = heads // tile_heads

    @pl.loop(0, 2)
    def _(which):
        block = meta_ref[which]
        if not first:
            for copy in half_copies(which, state_in, state, in_sem):
                copy.wait()

        def update(taken, masked):
            keys_len = len(taken) * unit_rows
            starts = [pl.multiple_of(unit * unit_rows, unit_rows) for unit in taken]
            keys = jnp.concatenate([kv_ref[pl.ds(s, unit_rows), :DH] for s in starts], axis=0)
            vals = jnp.concatenate([kv_ref[pl.ds(s, unit_rows), DH:] for s in starts], axis=0)
            if masked:
                shape = (BLOCK, unit_rows)
                row_token = lax.broadcasted_iota(jnp.int32, shape, 0)
                key_token = lax.broadcasted_iota(jnp.int32, shape, 1)
                ahead = (base_ref[taken[0]] - block) * BLOCK
                allowed = key_token + ahead <= row_token

            def scores_of(part):
                query = jnp.concatenate(
                    [
                        q_ref[which, :, pl.ds((part * tile_heads + h) * DH, DH)]
                        for h in range(tile_heads)
                    ],
                    axis=0,
                )
                scores = lax.dot_general(
                    query, keys, (((1,), (1,)), ((), ())), preferred_element_type=F32
                )
                if masked:
                    scores = jnp.where(
                        allowed[None], scores.reshape(tile_heads, BLOCK, keys_len), -1e30
                    ).reshape(rows, keys_len)
                return scores

            def absorb(part, scores):
                start = pl.multiple_of((which * heads + part * tile_heads) * BLOCK, BLOCK)
                span = pl.ds(start, rows)
                old_max = max_ref[span, :]
                new_max = jnp.maximum(old_max, jnp.max(scores, axis=1, keepdims=True))
                decay = jnp.exp2((old_max - new_max) * factor)
                lane_sum = sum_ref[span, :] * decay
                weights = []
                for column in range(keys_len // DH):
                    some = scores[:, column * DH : (column + 1) * DH]
                    piece = jnp.exp2((some - new_max) * factor)
                    lane_sum = lane_sum + piece
                    weights.append(piece.astype(BF16))
                sum_ref[span, :] = lane_sum
                max_ref[span, :] = new_max
                added = jnp.dot(jnp.concatenate(weights, axis=1), vals, preferred_element_type=F32)
                acc_ref[span, :] = acc_ref[span, :] * decay + added

            scores = scores_of(0)
            for part in range(parts):
                later = scores_of(part + 1) if part + 1 < parts else None
                absorb(part, scores)
                scores = later

        count = jnp.int32(0)
        tail = jnp.int32(0)
        for unit in range(len(units)):
            base = base_ref[unit]
            list_ref[count] = unit
            tail_ref[tail] = unit
            count = count + jnp.where(base + UNIT <= block, 1, 0)
            tail = tail + jnp.where(jnp.logical_and(base <= block, block < base + UNIT), 1, 0)
        pairs = count // 2
        tail_ref[tail] = list_ref[jnp.maximum(count - 1, 0)]
        tail = tail + count - 2 * pairs

        @pl.loop(0, pairs)
        def _(step):
            update([list_ref[2 * step], list_ref[2 * step + 1]], False)

        @pl.loop(0, tail)
        def _(step):
            update([tail_ref[step]], True)

        if not last:
            for copy in half_copies(which, state, state_out, out_sem):
                copy.start()

    if not last:
        for which in range(2):
            for copy in half_copies(which, state, state_out, out_sem):
                copy.wait()
    if last:
        for head in range(2 * heads):
            span = pl.ds(head * BLOCK, BLOCK)
            total = jnp.sum(sum_ref[span, :], axis=1, keepdims=True)
            out_refs[head // heads][:, pl.ds(head % heads * DH, DH)] = (
                acc_ref[span, :] / total
            ).astype(BF16)


def attend(meta, units, theirs, own, pieces, state=None, last=False, tile_heads=TILE_HEADS):
    rows, width = own.shape
    heads = width // DH
    smem = pl.BlockSpec(memory_space=pltpu.SMEM)
    vmem = pl.BlockSpec(memory_space=pltpu.VMEM)
    anywhere = pl.BlockSpec(memory_space=pl.ANY)
    states = [(2 * heads * rows, DH)] * 3
    scratch = [pltpu.VMEM(shape, F32) for shape in states] + [
        pltpu.VMEM((len(units) * UNIT * BLOCK, 2 * DH), BF16),
        pltpu.VMEM((2, rows, width), BF16),
        pltpu.SMEM((len(units),), jnp.int32),
        pltpu.SMEM((len(units) + 1,), jnp.int32),
        pltpu.SMEM((len(units) + 2,), jnp.int32),
        pltpu.SemaphoreType.DMA((len(pieces),)),
        pltpu.SemaphoreType.DMA((2,)),
        pltpu.SemaphoreType.DMA((2, 3)),
        pltpu.SemaphoreType.DMA((2, 3)),
    ]
    if last:
        out_shape = [jax.ShapeDtypeStruct((rows, width), BF16)] * 2
    else:
        out_shape = [jax.ShapeDtypeStruct(shape, F32) for shape in states]
    state = [] if state is None else list(state)
    kernel = functools.partial(
        attend_kernel,
        units=units,
        pieces=len(pieces),
        heads=heads,
        tile_heads=tile_heads,
        first=not state,
        last=last,
    )
    keys_seen = len(units) * UNIT * BLOCK
    return pl.pallas_call(
        kernel,
        in_specs=[smem] + [anywhere] * (2 + len(pieces) + len(state)),
        out_specs=[vmem if last else anywhere] * len(out_shape),
        out_shape=out_shape,
        scratch_shapes=scratch,
        compiler_params=params(),
        cost_estimate=pl.CostEstimate(
            flops=4 * keys_seen * heads * rows * DH,
            bytes_accessed=keys_seen * 4 * DH,
            transcendentals=keys_seen * heads * rows,
        ),
        name="attend_last" if last else "attend_more" if state else "attend_first",
    )(meta, theirs, own, *pieces, *state)


def slots_of(ids_ref):
    shape = (BLOCK, BLOCK)
    expert = lax.broadcasted_iota(jnp.int32, shape, 0)
    named = jnp.zeros(shape, F32)
    for k in range(TOP):
        named = named + jnp.where(ids_ref[k : k + 1, :] == expert, 1.0, 0.0)
    earlier = jnp.where(
        lax.broadcasted_iota(jnp.int32, shape, 0) < lax.broadcasted_iota(jnp.int32, shape, 1),
        1.0,
        0.0,
    )
    counts = jnp.dot(named.astype(BF16), earlier.astype(BF16), preferred_element_type=F32)
    return named, jnp.where(named > 0.0, counts, -1.0)


def own_kernel(core_ref, own_ref, w_ref, out_ref):
    @pl.when(pl.program_id(0) == 0)
    def _():
        out_ref[...] = jnp.zeros_like(out_ref)

    depth = w_ref.shape[0]
    column = pl.ds(pl.multiple_of(pl.program_id(0) * depth, depth), depth)
    out_ref[...] += jnp.dot(own_ref[:, column], w_ref[...], preferred_element_type=F32)


def project_own(core, own, w_out, depth=512):
    rows, half = own.shape
    width = w_out.shape[1]
    steps = half // depth
    return pl.pallas_call(
        own_kernel,
        grid_spec=pltpu.PrefetchScalarGridSpec(
            num_scalar_prefetch=1,
            grid=(steps,),
            in_specs=[
                pl.BlockSpec((rows, half), lambda step, core_ref: (0, 0)),
                pl.BlockSpec((depth, width), lambda step, core_ref: (core_ref[0] * steps + step, 0)),
            ],
            out_specs=pl.BlockSpec((rows, width), lambda step, core_ref: (0, 0)),
        ),
        out_shape=jax.ShapeDtypeStruct((rows, width), F32),
        compiler_params=params("arbitrary"),
        cost_estimate=pl.CostEstimate(
            flops=2 * rows * half * width, bytes_accessed=2 * half * width, transcendentals=0
        ),
        name="project_own",
    )(core, own, w_out)


def torus_place(expert):
    zh, y, c = expert // 64, expert // 16 % 4, expert // 8 % 2
    zl, x = expert // 4 % 2, expert % 4
    return zh * 64 + zl * 32 + y * 8 + x * 2 + c


def plan_kernel(ids_ref, slot_ref, pick_ref, last_ref):
    slot = slots_of(ids_ref)[1]
    slot_ref[...] = slot
    wanted = lax.broadcasted_iota(jnp.int32, (BLOCK, MAIN, BLOCK), 1).astype(F32)
    pick = jnp.where(slot[:, None, :] == wanted, 1.0, 0.0).reshape(BLOCK * MAIN, BLOCK)
    pick_ref[...] = pick.astype(BF16)
    last_ref[...] = jnp.where(slot == float(MAIN), 1.0, 0.0).astype(BF16)


def plan(places_t):
    rows = places_t.shape[1]
    vmem = pl.BlockSpec(memory_space=pltpu.VMEM)
    return pl.pallas_call(
        plan_kernel,
        in_specs=[vmem],
        out_specs=[vmem] * 3,
        out_shape=[
            jax.ShapeDtypeStruct((BLOCKS, rows), F32),
            jax.ShapeDtypeStruct((BLOCKS * MAIN, rows), BF16),
            jax.ShapeDtypeStruct((BLOCKS, rows), BF16),
        ],
        compiler_params=params(),
        name="plan",
    )(places_t)


def routes_kernel(hn_ref, router_ref, ids_ref, slot_ref, mix_ref, last_ref):
    logits = jnp.dot(hn_ref[...], router_ref[...], preferred_element_type=F32)
    named = slots_of(ids_ref)[0]
    raised = jnp.where(named > 0.0, jnp.exp(jnp.transpose(logits)), 0.0)
    by_expert = (raised / jnp.sum(raised, axis=0, keepdims=True)).astype(BF16)
    shape = (BLOCK, BLOCK)
    place = torus_place(lax.broadcasted_iota(jnp.int32, shape, 1))
    order = jnp.where(place == lax.broadcasted_iota(jnp.int32, shape, 0), 1.0, 0.0)
    route = jnp.dot(order.astype(BF16), by_expert, preferred_element_type=F32)
    slot = slot_ref[...]
    wanted = lax.broadcasted_iota(jnp.int32, (BLOCK, MAIN, BLOCK), 1).astype(F32)
    mix = jnp.where(slot[:, None, :] == wanted, route[:, None, :], 0.0)
    mix_ref[...] = jnp.transpose(mix.reshape(BLOCK * MAIN, BLOCK).astype(BF16))
    last_ref[...] = jnp.transpose(jnp.where(slot == float(MAIN), route, 0.0)).astype(BF16)


def routes(hn, w_router, ids_t, slot):
    rows = hn.shape[0]
    vmem = pl.BlockSpec(memory_space=pltpu.VMEM)
    return pl.pallas_call(
        routes_kernel,
        in_specs=[vmem] * 4,
        out_specs=[vmem] * 2,
        out_shape=[
            jax.ShapeDtypeStruct((rows, BLOCKS * MAIN), BF16),
            jax.ShapeDtypeStruct((rows, BLOCKS), BF16),
        ],
        compiler_params=params(),
        name="routes",
    )(hn, w_router, ids_t, slot)


def project_kernel(
    core_ref, part_ref, got_ref, w_ref, hidden_ref, gain_ref, pick_ref, last_ref,
    h1_ref, hn_ref, send_ref, acc_ref, over_ref, *, steps,
):
    step = pl.program_id(0)
    depth = w_ref.shape[0]
    tiles = hn_ref.shape[1] // DH

    @pl.when(step == 0)
    def _():
        acc_ref[...] = part_ref[...] + hidden_ref[...].astype(F32)

    @pl.when(step < steps)
    def _():
        column = pl.ds(pl.multiple_of(step * depth, depth), depth)
        acc_ref[...] += jnp.dot(got_ref[:, column], w_ref[...], preferred_element_type=F32)

    @pl.when(step == steps - 1)
    def _():
        h1 = acc_ref[...].astype(BF16)
        h1_ref[...] = h1
        h1_f = h1.astype(F32)
        mean = jnp.mean(h1_f * h1_f, axis=-1, keepdims=True)
        hn = (h1_f / jnp.sqrt(mean + 1e-06) * gain_ref[...]).astype(BF16)
        hn_ref[...] = hn
        for tile in range(tiles):
            part = hn[:, tile * DH : (tile + 1) * DH]
            over_ref[:, tile, :] = jnp.dot(last_ref[...], part, preferred_element_type=F32)

    stripe = send_ref.shape[1] // MAIN
    for index in range(pl.cdiv(tiles, stripe)):

        @pl.when(step == steps + index)
        def _(index=index):
            first = index * stripe
            held = min(stripe, tiles - first)
            columns = hn_ref[:, first * DH : (first + held) * DH]
            rows = jnp.dot(pick_ref[...], columns, preferred_element_type=F32)
            send_ref[:, : held * MAIN, :] = tiled_rows(rows)
            if held < stripe:
                send_ref[:, held * MAIN :, :] = over_ref[...].astype(BF16)


def tiled_rows(rows):
    sources = rows.shape[0] // MAIN
    pieces = [
        rows[:, tile * DH : (tile + 1) * DH].reshape(sources, MAIN, DH)
        for tile in range(rows.shape[1] // DH)
    ]
    return jnp.concatenate(pieces, axis=1).astype(BF16)


def project(core, part, got, w_out, hidden, gain, pick, last, depth=512):
    rows, half = got.shape
    width = hidden.shape[1]
    steps = half // depth
    experts = last.shape[0]
    tiles = width // DH
    packed = (experts, tiles * CAP, DH)

    def full(shape):
        return pl.BlockSpec(shape, lambda step, core_ref: (0,) * len(shape))

    def w_map(step, core_ref):
        return (1 - core_ref[0]) * steps + jnp.minimum(step, steps - 1), 0

    return pl.pallas_call(
        functools.partial(project_kernel, steps=steps),
        grid_spec=pltpu.PrefetchScalarGridSpec(
            num_scalar_prefetch=1,
            grid=(steps + packed[1] // STRIPE,),
            in_specs=[
                full((rows, width)),
                full((rows, half)),
                pl.BlockSpec((depth, width), w_map),
                full((rows, width)),
                full((1, width)),
                full(pick.shape),
                full(last.shape),
            ],
            out_specs=[
                full((rows, width)),
                full((rows, width)),
                pl.BlockSpec(
                    (experts, STRIPE, DH),
                    lambda step, core_ref: (0, jnp.maximum(step - steps, 0), 0),
                ),
            ],
            scratch_shapes=[
                pltpu.VMEM((rows, width), F32),
                pltpu.VMEM((experts, tiles, DH), F32),
            ],
        ),
        out_shape=[
            jax.ShapeDtypeStruct((rows, width), BF16),
            jax.ShapeDtypeStruct((rows, width), BF16),
            jax.ShapeDtypeStruct(packed, BF16),
        ],
        compiler_params=params("arbitrary"),
        name="project",
    )(core, part, got, w_out, hidden, gain, pick, last)


def expert_kernel(
    in_ref, gate_ref, up_ref, down_ref, out_ref, rows_ref, act_ref, over_ref, *, steps, up_steps
):
    step = pl.program_id(0)
    tile = gate_ref.shape[1]
    sources = in_ref.shape[0]
    main_rows = sources * MAIN
    tiles = gate_ref.shape[0] // DH
    stripe = in_ref.shape[1] // MAIN
    third = sources * CAP // 3

    for index in range(steps):

        @pl.when(step == index)
        def _(index=index):
            first = index * stripe
            held = min(stripe, tiles - first)
            for place in range(held):
                columns = pl.ds((first + place) * DH, DH)
                rows_ref[:main_rows, columns] = in_ref[
                    :, place * MAIN : (place + 1) * MAIN, :
                ].reshape(main_rows, DH)
            if held < stripe:
                over_ref[...] = in_ref[:, held * MAIN :, :].astype(F32)
                for place in range(tiles):
                    columns = pl.ds(place * DH, DH)
                    rows_ref[main_rows:, columns] = over_ref[:, place, :].astype(BF16)

    for index in range(up_steps):

        @pl.when(step == steps + index)
        def _(index=index):
            for start in range(0, 3 * third, third):
                rows = rows_ref[start : start + third, :]
                gate = jnp.dot(rows, gate_ref[...], preferred_element_type=F32)
                up = jnp.dot(rows, up_ref[...], preferred_element_type=F32)
                act = gate / (1.0 + jnp.exp(-gate)) * up
                act_ref[start : start + third, index * tile : (index + 1) * tile] = act.astype(BF16)

    for index in range(steps):

        @pl.when(step == steps + up_steps + index)
        def _(index=index):
            first = index * stripe
            held = min(stripe, tiles - first)
            for start in range(0, 3 * third, third):
                rows = jnp.dot(
                    act_ref[start : start + third, :],
                    down_ref[:, : held * DH],
                    preferred_element_type=F32,
                )
                some = min(third, main_rows - start)
                out_ref[start // MAIN : (start + some) // MAIN, : held * MAIN, :] = tiled_rows(
                    rows[:some]
                )
                if some < third:
                    for place in range(held):
                        over_ref[:, first + place, :] = rows[some:, place * DH : (place + 1) * DH]
            if held < stripe:
                out_ref[:, held * MAIN :, :] = over_ref[...].astype(BF16)


def experts_of(packed, w_gate, w_up, w_down):
    sources = packed.shape[0]
    width, hidden_units = w_gate.shape
    tile = 256
    steps = packed.shape[1] // STRIPE
    up_steps = hidden_units // tile
    rows = sources * CAP

    def out_step(step):
        return jnp.maximum(step - steps - up_steps, 0)

    def up_map(step):
        return 0, jnp.clip(step - steps, 0, up_steps - 1)

    return pl.pallas_call(
        functools.partial(expert_kernel, steps=steps, up_steps=up_steps),
        grid=(2 * steps + up_steps,),
        in_specs=[
            pl.BlockSpec((sources, STRIPE, DH), lambda step: (0, jnp.minimum(step, steps - 1), 0)),
            pl.BlockSpec((width, tile), up_map),
            pl.BlockSpec((width, tile), up_map),
            pl.BlockSpec((hidden_units, STRIPE // MAIN * DH), lambda step: (0, out_step(step))),
        ],
        out_specs=pl.BlockSpec((sources, STRIPE, DH), lambda step: (0, out_step(step), 0)),
        out_shape=jax.ShapeDtypeStruct(packed.shape, BF16),
        scratch_shapes=[
            pltpu.VMEM((rows, width), BF16),
            pltpu.VMEM((rows, hidden_units), BF16),
            pltpu.VMEM((sources, width // DH, DH), F32),
        ],
        compiler_params=params("arbitrary"),
        name="experts_of",
    )(packed, w_gate, w_up, w_down)


def combine_kernel(
    mix_ref, last_ref, in_ref, in_over_ref, h1_ref, out_ref, over_ref, *, tiles
):
    step = pl.program_id(0)
    stripe = in_ref.shape[1] // MAIN

    @pl.when(step == 0)
    def _():
        over_ref[...] = in_over_ref[...].astype(F32)

    for index in range(pl.cdiv(tiles, stripe)):

        @pl.when(step == index)
        def _(index=index):
            first = index * stripe
            held = min(stripe, tiles - first)
            rows = jnp.concatenate(
                [
                    in_ref[:, p * MAIN : (p + 1) * MAIN, :].reshape(BLOCK * MAIN, DH)
                    for p in range(held)
                ],
                axis=1,
            )
            extra = jnp.concatenate(
                [over_ref[:, first + p, :].astype(BF16) for p in range(held)], axis=1
            )
            total = jnp.dot(mix_ref[...], rows, preferred_element_type=F32)
            total = total + jnp.dot(last_ref[...], extra, preferred_element_type=F32)
            columns = slice(first * DH, (first + held) * DH)
            out_ref[:, columns] = (total + h1_ref[:, columns].astype(F32)).astype(BF16)


def combine(mix, last, packed, h1):
    rows, width = h1.shape
    experts = packed.shape[0]
    tiles = width // DH

    def whole(shape):
        return pl.BlockSpec(shape, lambda step: (0,) * len(shape))

    return pl.pallas_call(
        functools.partial(combine_kernel, tiles=tiles),
        grid=(packed.shape[1] // STRIPE,),
        in_specs=[
            whole(mix.shape),
            whole(last.shape),
            pl.BlockSpec((experts, STRIPE, DH), lambda step: (0, step, 0)),
            pl.BlockSpec((experts, tiles, DH), lambda step: (0, MAIN, 0)),
            whole(h1.shape),
        ],
        out_specs=whole(h1.shape),
        out_shape=jax.ShapeDtypeStruct((rows, width), BF16),
        scratch_shapes=[pltpu.VMEM((experts, tiles, DH), F32)],
        compiler_params=params("arbitrary"),
        name="combine",
    )(mix, last, packed, packed, h1)


def exchange(packed):
    return lax.all_to_all(packed, TORUS, split_axis=0, concat_axis=0, tiled=True)


def ring_step(piece, axes, by):
    return lax.ppermute(piece, axes, [(i, (i + by) % 4) for i in range(4)])


def ring_gather(piece, axes):
    left, right, far = (ring_step(piece, axes, by) for by in (1, 3, 2))
    return jnp.concatenate([piece, left], axis=0), jnp.concatenate([right, far], axis=0)


def ring_near(halves, axes):
    top, bottom = halves
    left_top, right_bottom = ring_step(top, axes, 1), ring_step(bottom, axes, 3)
    left_bottom, right_top = ring_step(bottom, axes, 1), ring_step(top, axes, 3)
    return left_top, left_bottom, right_top, right_bottom


def ring_far(near, axes):
    return ring_step(near[0], axes, 1), ring_step(near[3], axes, 3)


def local(
    hidden, queries, keys, values, w_out, norm_gain, w_router, expert_ids, w_gate, w_up, w_down
):
    rows = hidden.shape[0]
    device = lax.axis_index(AXES)
    core = lax.axis_index("c")
    positions = device * rows + jnp.arange(rows, dtype=jnp.int32)
    cos_t, sin_t = yarn_tables(positions, DH)
    core_arr = core.reshape(1).astype(jnp.int32)
    keep, give, keep_kv, give_kv = rotate_all(core_arr, queries, keys, values, cos_t, sin_t)
    mirror = [(i, BLOCKS - 1 - i) for i in range(BLOCKS)]
    taken = lax.ppermute(give, AXES, mirror)
    other_kv = lax.ppermute(give_kv, ("c",), [(0, 1), (1, 0)])
    is_low = core == 0
    chip = jnp.concatenate(
        [jnp.where(is_low, keep_kv, other_kv), jnp.where(is_low, other_kv, keep_kv)], axis=0
    )
    row = lax.all_gather(chip, ("x",), axis=0)
    low = row[:, :rows].reshape(UNIT * rows, 2 * DH)
    high = row[:, rows:].reshape(UNIT * rows, 2 * DH)
    low = ring_gather(low, RING_Y)
    high = ring_gather(high, RING_Z)
    low_near = ring_near(low, RING_Z)
    high_near = ring_near(high, RING_Y)
    low_far = ring_far(low_near, RING_Z)
    high_far = ring_far(high_near, RING_Y)

    def units(order):
        return [(outer, inner, 0) for outer in order for inner in OFFSETS] + [
            (inner, outer, 1) for outer in order for inner in OFFSETS
        ]

    meta = jnp.stack(
        [BLOCKS - 1 - device, device, lax.axis_index(RING_Z), lax.axis_index(RING_Y)]
    ).astype(jnp.int32)
    state = attend(meta, units((0,)), taken, keep, [*low, *high])
    state = attend(meta, units((-1, 1)), taken, keep, [*low_near, *high_near], state=state)
    theirs, own = attend(
        meta, units((2,)), taken, keep, [*low_far, *high_far], state=state, last=True
    )
    got = lax.ppermute(theirs, AXES, mirror)
    part = project_own(core_arr, own, w_out)
    slot, pick, last = plan(torus_place(expert_ids.T))
    h1, hn, packed = project(
        core_arr, part, got, w_out, hidden, norm_gain[None, :], pick, last
    )
    arrived = exchange(packed)
    mix, last = routes(hn, w_router, expert_ids.T, slot)
    returned = exchange(experts_of(arrived, w_gate[0], w_up[0], w_down[0]))
    return combine(mix, last, returned, h1)


def solution(mesh):
    torus = Mesh(mesh.devices.reshape(2, 4, 2, 2, 4), AXES)
    split = P(AXES, None)
    experts = P(AXES, None, None)
    in_specs = (
        split, split, split, split, P(), P(), P(), split, experts, experts, experts,
    )
    return jax.shard_map(local, mesh=torus, in_specs=in_specs, out_specs=split, check_vma=False)
```
